32 devices in a mesh: sec: 4 (over y, x), col: 8 (over z, core).
Axes of the slice: x: 2, y: 2, z: 4, core: 2. Of those that a mesh axis runs over, the one named last changes fastest.
Arguments:
- state: float32 [16384, 7, 64], P(('sec', 'col')), may hold values from -6 to 6
- cosine: float32 [16384], P(('sec', 'col')), may hold values from 0.05 to 1
- grouping: int32 [32, 512], P(('sec', 'col')), may hold values from 0 to 511, each once within a row
- sunlit: int32 [32], P(('sec', 'col')), may hold values from 0 to 128
- absorb: float32 [256, 64, 448], P('sec'), may hold values from -0.25 to 0.25
- level_bias: float32 [256, 64], P('sec'), may hold values from -4 to 2
- planck: float32 [256], P('sec'), may hold values from 0.2 to 2
- solar_share: float32 [256], P('sec'), may hold values from 0.2 to 2
- stencil: int32 [3, 16384], P(None, ('sec', 'col')), may hold values from 0 to 143, as said below
- stencil_weight: float32 [3, 16384], P(None, ('sec', 'col')), may hold values from 0 to 1
Outputs:
- heating: float32 [64, 16384], P(None, ('sec', 'col'))
The draws below stay inside these ranges and needn't reach their ends.
Inputs may be any that keep to these rules, and one draw needn't show every extreme that they name: Each row of grouping is a permutation of 0..511. stencil[k, p] lies within 8 of (p mod 512) // 4 + 8.
All inputs are finite; a program needn't handle non-finite values.
Results may differ from the reference program's by a relative error of at most 0.00007.
Values sent between devices are 32-bit elements; how exact they have to be, the bound alone decides.
No kernel may reach another device: no remote copies, remote signals or barrier semaphores. Data moves between devices by JAX's collectives and lax.ppermute only.
A program may use at most 128 MiB of HBM per device.

```python
import math
import jax
import jax.numpy as jnp
from jax import lax

G = 256
FIELDS = 7
LEV = 64
FEAT = 448
RIM = 8
F_DEV = 512
C_DEV = 128
FINE = 16384
COARSE = 4096
DEVICES = 32


def draw_sunlit(key, part):
    count = COARSE // 128
    first, second = jax.random.split(key)
    place = jnp.arange(count, dtype=jnp.int32)
    day_side = jax.random.randint(first, (count,), 64, 129)
    night_side = jax.random.randint(second, (count,), 0, 65)
    counts = jnp.where(place < count // 2, day_side, night_side)
    counts = counts.at[0].set(128).at[count - 1].set(0)
    return counts.astype(jnp.int32)


def draw_stencil(key, part):
    place = jnp.arange(FINE, dtype=jnp.int32)
    local = place % F_DEV
    home = local // 4 + RIM
    offsets = jax.random.randint(key, (3, FINE), -RIM, RIM + 1)
    edge = jnp.where(local == 0, -RIM, jnp.where(local == F_DEV - 1, RIM, offsets[0]))
    offsets = offsets.at[0].set(edge)
    return (home[None, :] + offsets).astype(jnp.int32)


def level_of(own_key, shape, cuts, smallest, top_value):
    factor_of, own = 1.0, jax.random.fold_in(own_key, 6)
    for axis_at, parts in cuts:
        draws = jnp.exp(jax.random.uniform(jax.random.fold_in(own, axis_at), (parts,), jnp.float32, smallest / len(cuts), top_value / len(cuts)))
        factor_of = factor_of * jnp.repeat(draws, shape[axis_at] // parts).reshape([-1 if axis == axis_at else 1 for axis in range(len(shape))])
    return factor_of


def gaussian(own_key, dims, deviation, bound, cuts=(), kind=jnp.bfloat16):
    level = level_of(own_key, dims, cuts, -0.22, 0.18) if cuts else 1.0
    array = jax.random.normal(own_key, dims, jnp.float32) * deviation * level
    return jnp.minimum(jnp.maximum(array, -bound), bound).astype(kind)


def setup_inputs(seed: int = 0) -> dict:
    splits = jax.random.split(jax.random.key(seed), 11)
    state = gaussian(splits[0], (FINE, FIELDS, LEV), 1.0, 6.0, ((0, 32),), jnp.float32)
    cosine = jnp.clip(0.05 + 0.95 * jax.random.uniform(splits[1], (FINE,), jnp.float32) ** level_of(splits[1], (FINE,), ((0, 32),), -0.2, 0.2), 0.05, 1.0)
    grouping = jax.vmap(lambda own: jax.random.permutation(own, F_DEV))(jax.random.split(splits[2], DEVICES)).reshape((DEVICES, F_DEV)).astype(jnp.int32)
    sunlit = draw_sunlit(jax.random.fold_in(splits[10], 71), 0)
    absorb = gaussian(splits[4], (G, LEV, FEAT), FEAT ** -0.5, 0.25, ((0, 4),), jnp.float32)
    level_bias = jnp.clip(-4.0 + 6.0 * jax.random.uniform(splits[5], (G, LEV), jnp.float32) ** level_of(splits[5], (G, LEV), ((0, 4),), -0.2, 0.2), -4.0, 2.0)
    planck = jnp.clip(jnp.exp(math.log(2.0) - 2.3025851 * jax.random.uniform(splits[6], (G,), jnp.float32) ** level_of(splits[6], (G,), ((0, 4),), -0.2, 0.2)), 0.2, 2.0)
    solar_share = jnp.clip(jnp.exp(math.log(2.0) - 2.3025851 * jax.random.uniform(splits[7], (G,), jnp.float32) ** level_of(splits[7], (G,), ((0, 4),), -0.2, 0.2)), 0.2, 2.0)
    stencil = draw_stencil(jax.random.fold_in(splits[10], 71), 0)
    stencil_weight = jnp.clip(1.0 * jax.random.uniform(splits[9], (3, FINE), jnp.float32) ** level_of(splits[9], (3, FINE), ((1, 32),), -0.2, 0.2), 0.0, 1.0)
    return dict(state=state, cosine=cosine, grouping=grouping, sunlit=sunlit, absorb=absorb, level_bias=level_bias, planck=planck, solar_share=solar_share, stencil=stencil, stencil_weight=stencil_weight)


def radiate(rows, solar, absorb, level_bias, planck, solar_share):
    levels = level_bias.shape[1]
    z = jnp.einsum('glk,mk->glm', absorb, rows, precision=lax.Precision.HIGHEST) + level_bias[:, :, None]
    trans = jnp.exp(-0.1 * jax.nn.softplus(z))
    warm = 2.0 + jnp.tanh(rows[:, :levels].T)
    source = (1.0 - trans) * planck[:, None, None] * warm[None]
    top = solar_share[:, None] * solar[None, :]

    def advance(carry, pair):
        value = pair[0] * carry + pair[1]
        return value, value

    steps_in = (jnp.moveaxis(trans, 1, 0), jnp.moveaxis(source, 1, 0))
    _, lower = lax.scan(advance, top, steps_in)
    fall = jnp.concatenate([top[None], lower], axis=0)
    bottom = 0.3 * fall[-1] + planck[:, None] * warm[-1][None]
    _, upper = lax.scan(advance, bottom, steps_in, reverse=True)
    rise = jnp.concatenate([upper, bottom[None]], axis=0)
    net = fall - rise
    return (4.0 / G) * jnp.sum(net[:-1] - net[1:], axis=1)


def reference(state, cosine, grouping, sunlit, absorb, level_bias, planck, solar_share, stencil, stencil_weight):
    base = (jnp.arange(DEVICES, dtype=jnp.int32) * F_DEV)[:, None]
    picks = (grouping + base).reshape(-1)
    grouped = state[picks]
    rows = grouped.reshape(COARSE, 4, FEAT).mean(axis=1)
    bright = cosine[picks].reshape(COARSE, 4).mean(axis=1)
    lit = (jnp.arange(128, dtype=jnp.int32)[None, :] < sunlit[:, None]).reshape(COARSE)
    solar = jnp.where(lit, 4.0 * bright, 0.0)

    def one_block(pair):
        return radiate(pair[0], pair[1], absorb, level_bias, planck, solar_share)

    heat = lax.map(one_block, (rows.reshape(DEVICES, C_DEV, FEAT), solar.reshape(DEVICES, C_DEV)))
    coarse_heat = jnp.moveaxis(heat, 0, 1).reshape(LEV, COARSE)
    owner = jnp.arange(FINE, dtype=jnp.int32) // F_DEV
    total = jnp.zeros((LEV, FINE), jnp.float32)
    for k in range(3):
        index = (owner * C_DEV + stencil[k] - RIM) % COARSE
        total = total + stencil_weight[k][None, :] * jnp.take(coarse_heat, index, axis=1)
    return total
```

```python
import functools

import jax
import jax.numpy as jnp
from jax import lax
from jax.experimental import pallas as pl
from jax.experimental.pallas import tpu as pltpu
from jax.sharding import PartitionSpec as P

RIM = 8
MIB = 1 << 20
bf16 = jnp.bfloat16
f32 = jnp.float32
VMEM = pl.BlockSpec(memory_space=pltpu.VMEM)


def split(x, parts):
    terms = []
    for _ in range(parts):
        term = x.astype(bf16)
        terms.append(term)
        x = x - term.astype(f32)
    return terms


def dot(a, b):
    return jnp.dot(a, b, preferred_element_type=f32)


def group_body(state, cosine, grouping, sunlit, out):
    feat, fine = state.shape
    coarse = out.shape[1]
    place = lax.broadcasted_iota(jnp.int32, (fine, fine), 0)
    picks = jnp.where(place == grouping[...], 1.0, 0.0).astype(bf16)
    member = lax.broadcasted_iota(jnp.int32, (fine, coarse), 0) // 4
    home = lax.broadcasted_iota(jnp.int32, (fine, coarse), 1)
    mean = jnp.where(member == home, 0.25, 0.0).astype(bf16)
    weights = dot(picks, mean).astype(bf16)
    total = jnp.zeros((feat, coarse), f32)
    for term in split(state[...], 3)[::-1]:
        total = total + dot(term, weights)
    out[0:feat, :] = total
    light = jnp.zeros((8, coarse), f32)
    for term in split(jnp.broadcast_to(cosine[...], (8, fine)), 3)[::-1]:
        light = light + dot(term, weights)
    lane = lax.broadcasted_iota(jnp.int32, (8, coarse), 1)
    out[feat : feat + 8, :] = jnp.where(lane < sunlit[0], 4.0 * light, 0.0)


def group(state, cosine, grouping, sunlit):
    feat, fine = state.shape
    coarse = fine // 4
    return pl.pallas_call(
        group_body,
        out_shape=jax.ShapeDtypeStruct((feat + 8, coarse), f32),
        in_specs=[VMEM, VMEM, VMEM, pl.BlockSpec(memory_space=pltpu.SMEM)],
        out_specs=VMEM,
        compiler_params=pltpu.CompilerParams(vmem_limit_bytes=16 * MIB),
        cost_estimate=pl.CostEstimate(
            flops=8 * feat * fine * coarse, bytes_accessed=4 * feat * fine, transcendentals=0
        ),
        name="group",
    )(state, cosine, grouping, sunlit)


def tables_body(planck, share, stencil, weight, planck_out, share_out, high, low):
    def column(row):
        n = row.shape[1]
        eye = lax.broadcasted_iota(jnp.int32, (n, n), 0) == lax.broadcasted_iota(
            jnp.int32, (n, n), 1
        )
        return jnp.sum(jnp.where(eye, row, 0.0), axis=1, keepdims=True)

    planck_out[...] = jnp.broadcast_to(column(planck[...]), planck_out.shape)
    share_out[...] = jnp.broadcast_to(column(share[...]), share_out.shape)
    wide, fine = high.shape
    coarse = wide // 2
    place = lax.broadcasted_iota(jnp.int32, (wide, fine), 0)
    total = jnp.zeros((wide, fine), f32)
    for k in range(stencil.shape[0]):
        at = stencil[k : k + 1, :]
        spot = jnp.where(
            at < RIM,
            2 * coarse - RIM + at,
            jnp.where(at < coarse + RIM, at - RIM, at - RIM),
        )
        total = total + jnp.where(place == spot, weight[k : k + 1, :], 0.0)
    parts = split(total, 2)
    high[...] = parts[0]
    low[...] = parts[1]


def tables(planck, share, stencil, weight, coarse):
    g = planck.shape[1]
    fine = stencil.shape[1]
    column = jax.ShapeDtypeStruct((g, coarse), f32)
    table = jax.ShapeDtypeStruct((2 * coarse, fine), bf16)
    return pl.pallas_call(
        tables_body,
        out_shape=(column, column, table, table),
        in_specs=[VMEM] * 4,
        out_specs=[VMEM] * 4,
        compiler_params=pltpu.CompilerParams(vmem_limit_bytes=16 * MIB),
        cost_estimate=pl.CostEstimate(
            flops=20 * coarse * fine, bytes_accessed=8 * coarse * fine, transcendentals=0
        ),
        name="tables",
    )(planck, share, stencil, weight)


def prepare_body(absorb, bias, high, low):
    i = pl.program_id(0)
    count = absorb.shape[1]
    b = bias[...]
    lane = lax.broadcasted_iota(jnp.int32, b.shape, 1)
    for j in range(count):
        tail = jnp.where(lane == i * count + j, b, 0.0)
        parts = split(jnp.concatenate([absorb[:, j, :], tail], axis=1), 2)
        high[j] = parts[0]
        low[j] = parts[1]


def prepare(absorb, bias):
    g, levels, feat = absorb.shape
    block = 8
    depth = feat + levels
    table = jax.ShapeDtypeStruct((levels, g, depth), bf16)
    spec = pl.BlockSpec((block, g, depth), lambda i: (i, 0, 0))
    return pl.pallas_call(
        prepare_body,
        out_shape=(table, table),
        grid=(levels // block,),
        in_specs=[
            pl.BlockSpec((g, block, feat), lambda i: (0, i, 0)),
            pl.BlockSpec((g, levels), lambda i: (0, 0)),
        ],
        out_specs=[spec, spec],
        compiler_params=pltpu.CompilerParams(vmem_limit_bytes=16 * MIB),
        cost_estimate=pl.CostEstimate(
            flops=10 * g * levels * feat, bytes_accessed=8 * g * levels * depth, transcendentals=0
        ),
        name="prepare",
    )(absorb, bias)


def trans_of(z):
    low = jnp.log(1.0 + jnp.exp(jnp.minimum(z, 40.0)))
    return jnp.exp(-0.1 * jnp.maximum(low, z))


def flux_body(block, scale, high, low, rows, planck, share, out, right, zs, ts, downs, warms):
    levels, g, depth = high.shape
    feat = depth - levels
    n = rows.shape[1]
    blocks = levels // block
    parts = split(rows[0:feat, :], 2)
    right[0:feat, 0:n] = parts[0]
    right[0:feat, n : 2 * n] = parts[1]
    right[feat:depth, 0:n] = jnp.ones((levels, n), bf16)
    right[feat:depth, n : 2 * n] = jnp.zeros((levels, n), bf16)
    warms[0:levels, :] = 2.0 + jnp.tanh(rows[0:levels, :])
    warms[levels : levels + 8, :] = jnp.zeros((8, n), f32)
    weight = planck[...]

    def fold(x):
        return jnp.sum(x.reshape(g // 8, 8, n), axis=0)

    def absorb(b, slot):
        a = high[pl.ds(b * block, block)].reshape(block * g, depth)
        c = low[pl.ds(b * block, block)].reshape(block * g, depth)
        z = dot(a, right[...]) + dot(c, right[...])
        zs[slot] = z[:, 0:n] + z[:, n : 2 * n]

    def fall(b, slot, d):
        for j in range(block):
            l = b * block + j
            t = trans_of(zs[slot, j * g : (j + 1) * g, :])
            ts[l] = t
            d = t * d + weight * (warms[pl.ds(l, 1), :] - warms[pl.ds(l + 1, 1), :])
            downs[l + 1] = fold(d)
        return d

    d = share[...] * rows[feat : feat + 1, :] - weight * warms[0:1, :]
    downs[0] = fold(d)
    absorb(0, 0)

    def step(i, d):
        absorb(2 * i + 1, 1)
        d = fall(2 * i, 0, d)
        absorb(jnp.minimum(2 * i + 2, blocks - 1), 0)
        return fall(2 * i + 1, 1, d)

    d = lax.fori_loop(0, blocks // 2, step, d)
    total = jnp.sum(fold(weight), axis=0, keepdims=True)
    v = 0.3 * d

    def climb(i, carry):
        v, below = carry
        l = levels - 1 - i
        here = warms[pl.ds(l, 1), :]
        rise = here - warms[pl.ds(jnp.maximum(l - 1, 0), 1), :]
        v = ts[l] * v + weight * rise
        above = fold(v)
        part = (downs[l] - downs[l + 1]) + (below - above)
        row = jnp.sum(part, axis=0, keepdims=True)
        row = row + total * ((here - warms[pl.ds(l + 1, 1), :]) + rise)
        out[pl.ds(l, 1), :] = scale * row
        return v, above

    lax.fori_loop(0, levels, climb, (v, fold(v)), unroll=4)


def flux(high, low, rows, planck, share, scale):
    levels, g, depth = high.shape
    n = rows.shape[1]
    block = 4
    return pl.pallas_call(
        functools.partial(flux_body, block, scale),
        out_shape=jax.ShapeDtypeStruct((levels, n), f32),
        in_specs=[VMEM] * 5,
        out_specs=VMEM,
        scratch_shapes=[
            pltpu.VMEM((depth, 2 * n), bf16),
            pltpu.VMEM((2, block * g, n), f32),
            pltpu.VMEM((levels, g, n), f32),
            pltpu.VMEM((levels + 1, 8, n), f32),
            pltpu.VMEM((levels + 8, n), f32),
        ],
        compiler_params=pltpu.CompilerParams(vmem_limit_bytes=16 * MIB),
        cost_estimate=pl.CostEstimate(
            flops=8 * g * levels * depth * n,
            bytes_accessed=4 * g * levels * depth,
            transcendentals=3 * g * levels * n,
        ),
        name="flux",
    )(high, low, rows, planck, share)


def spread_body(own, first, second, parity, high, low, out):
    n = own.shape[1]
    lane = lax.broadcasted_iota(jnp.int32, own.shape, 1)
    late = jnp.where(lane >= n // 2, 1, 0)
    halo = jnp.where(late == parity[0], first[...], second[...])
    wide = jnp.concatenate([own[...], halo], axis=1)
    a, c = split(wide, 2)
    out[...] = dot(a, high[...]) + (dot(a, low[...]) + dot(c, high[...]))


def spread(own, first, second, parity, high, low):
    levels = own.shape[0]
    fine = high.shape[1]
    return pl.pallas_call(
        spread_body,
        out_shape=jax.ShapeDtypeStruct((levels, fine), f32),
        in_specs=[VMEM] * 3 + [pl.BlockSpec(memory_space=pltpu.SMEM)] + [VMEM] * 2,
        out_specs=VMEM,
        compiler_params=pltpu.CompilerParams(vmem_limit_bytes=16 * MIB),
        name="spread",
    )(own, first, second, parity, high, low)


def shards(
    state, cosine, grouping, sunlit, absorb, level_bias, planck, solar_share, stencil, stencil_weight
):
    fine, fields, levels = state.shape
    coarse = fine // 4
    n_sec = lax.axis_size("sec")
    devices = n_sec * lax.axis_size("col")
    columns = state.transpose(1, 2, 0).reshape(fields * levels, fine)
    rows = group(columns, cosine[None], grouping, sunlit)

    def swap(x, m):
        return lax.ppermute(x, "sec", [(i, i ^ m) for i in range(n_sec)])

    got = {m: swap(rows, m) for m in range(1, n_sec)}
    high, low = prepare(absorb, level_bias)
    weight, share, near, far = tables(planck[None], solar_share[None], stencil, stencil_weight, coarse)
    scale = 4.0 / (planck.shape[0] * n_sec)
    back = {}
    for m in range(1, n_sec):
        part = flux(high, low, got[m], weight, share, scale)
        back[m] = swap(part, m)
    total = flux(high, low, rows, weight, share, scale)
    for m in range(1, n_sec):
        total = total + back[m]
    pairs = [(i, i ^ 1) for i in range(devices)]
    across = [(i, (i + 1) % devices if i % 2 else (i - 1) % devices) for i in range(devices)]
    second = lax.ppermute(total, ("sec", "col"), across)
    first = lax.ppermute(total, ("sec", "col"), pairs)
    parity = (lax.axis_index(("sec", "col")) % 2).astype(jnp.int32).reshape(1)
    return spread(total, first, second, parity, near, far)


def solution(mesh):
    placed = (
        P(("sec", "col"), None, None),
        P(("sec", "col")),
        P(("sec", "col"), None),
        P(("sec", "col")),
        P("sec", None, None),
        P("sec", None),
        P("sec"),
        P("sec"),
        P(None, ("sec", "col")),
        P(None, ("sec", "col")),
    )
    return jax.shard_map(
        shards, mesh=mesh, in_specs=placed, out_specs=P(None, ("sec", "col")), check_vma=False
    )
```

```python
import functools

import jax
import jax.numpy as jnp
from jax import lax
from jax.experimental import pallas as pl
from jax.experimental.pallas import tpu as pltpu
from jax.sharding import PartitionSpec as P

RIM = 8
MIB = 1 << 20
bf16 = jnp.bfloat16
f32 = jnp.float32
VMEM = pl.BlockSpec(memory_space=pltpu.VMEM)


def split(x, parts):
    terms = []
    for _ in range(parts):
        term = x.astype(bf16)
        terms.append(term)
        x = x - term.astype(f32)
    return terms


def dot(a, b):
    return jnp.dot(a, b, preferred_element_type=f32)


HBM = pl.BlockSpec(memory_space=pltpu.HBM)


def stay(x):
    return pltpu.with_memory_space_constraint(x, pltpu.HBM)


def group_body(state_in, cosine_in, grouping_in, sunlit, out, state, cosine, grouping, sems):
    copies = [
        pltpu.make_async_copy(source, target, sems.at[i])
        for i, (source, target) in enumerate(
            ((grouping_in, grouping), (cosine_in, cosine), (state_in, state))
        )
    ]
    for copy in copies:
        copy.start()
    feat, fine = state.shape
    coarse = out.shape[1]
    place = lax.broadcasted_iota(jnp.int32, (fine, fine), 0)
    member = lax.broadcasted_iota(jnp.int32, (fine, coarse), 0) // 4
    home = lax.broadcasted_iota(jnp.int32, (fine, coarse), 1)
    mean = jnp.where(member == home, 0.25, 0.0).astype(bf16)
    copies[0].wait()
    picks = jnp.where(place == grouping[...], 1.0, 0.0).astype(bf16)
    weights = dot(picks, mean).astype(bf16)
    copies[1].wait()
    copies[2].wait()
    total = jnp.zeros((feat, coarse), f32)
    for term in split(state[...], 3)[::-1]:
        total = total + dot(term, weights)
    out[0:feat, :] = total
    light = jnp.zeros((8, coarse), f32)
    for term in split(jnp.broadcast_to(cosine[...], (8, fine)), 3)[::-1]:
        light = light + dot(term, weights)
    lane = lax.broadcasted_iota(jnp.int32, (8, coarse), 1)
    out[feat : feat + 8, :] = jnp.where(lane < sunlit[0], 4.0 * light, 0.0)


def group(state, cosine, grouping, sunlit):
    feat, fine = state.shape
    coarse = fine // 4
    return pl.pallas_call(
        group_body,
        out_shape=jax.ShapeDtypeStruct((feat + 8, coarse), f32),
        in_specs=[HBM, HBM, HBM, pl.BlockSpec(memory_space=pltpu.SMEM)],
        out_specs=VMEM,
        scratch_shapes=[
            pltpu.VMEM((feat, fine), f32),
            pltpu.VMEM((1, fine), f32),
            pltpu.VMEM((1, fine), jnp.int32),
            pltpu.SemaphoreType.DMA((3,)),
        ],
        compiler_params=pltpu.CompilerParams(vmem_limit_bytes=16 * MIB),
        cost_estimate=pl.CostEstimate(
            flops=8 * feat * fine * coarse, bytes_accessed=4 * feat * fine, transcendentals=0
        ),
        name="group",
    )(stay(state), stay(cosine), stay(grouping), sunlit)


def prepare_body(
    block,
    absorb_in,
    bias_in,
    planck_in,
    share_in,
    stencil_in,
    weight_in,
    table,
    planck_out,
    share_out,
    high,
    low,
    absorb,
    bias,
    planck,
    share,
    stencil,
    weight,
    sems,
):
    levels, g, double = table.shape
    depth = double // 2
    blocks = levels // block
    small = [
        pltpu.make_async_copy(source, target, sems.at[i])
        for i, (source, target) in enumerate(
            (
                (bias_in, bias),
                (planck_in, planck),
                (share_in, share),
                (stencil_in, stencil),
                (weight_in, weight),
            )
        )
    ]
    large = [
        pltpu.make_async_copy(
            absorb_in.at[:, pl.ds(i * block, block), :], absorb.at[i], sems.at[len(small) + i]
        )
        for i in range(blocks)
    ]
    for copy in small + large:
        copy.start()
    for copy in small:
        copy.wait()

    def column(row):
        n = row.shape[1]
        eye = lax.broadcasted_iota(jnp.int32, (n, n), 0) == lax.broadcasted_iota(
            jnp.int32, (n, n), 1
        )
        return jnp.sum(jnp.where(eye, row, 0.0), axis=1, keepdims=True)

    planck_out[...] = jnp.broadcast_to(column(planck[...]), planck_out.shape)
    share_out[...] = jnp.broadcast_to(column(share[...]), share_out.shape)
    wide, fine = high.shape
    place = lax.broadcasted_iota(jnp.int32, (wide, fine), 0)
    total = jnp.zeros((wide, fine), f32)
    for k in range(stencil.shape[0]):
        at = stencil[k : k + 1, :]
        spot = jnp.where(at < RIM, wide - RIM + at, at - RIM)
        total = total + jnp.where(place == spot, weight[k : k + 1, :], 0.0)
    parts = split(total, 2)
    high[...] = parts[0]
    low[...] = parts[1]

    b = bias[...]
    lane = lax.broadcasted_iota(jnp.int32, b.shape, 1)
    for i in range(blocks):
        large[i].wait()
        for j in range(block):
            tail = jnp.where(lane == i * block + j, b, 0.0)
            parts = split(jnp.concatenate([absorb[i, :, j, :], tail], axis=1), 2)
            table[i * block + j, :, 0:depth] = parts[0]
            table[i * block + j, :, depth:double] = parts[1]


def prepare(absorb, bias, planck, share, stencil, weight, coarse):
    g, levels, feat = absorb.shape
    fine = stencil.shape[1]
    block = 8
    depth = feat + levels
    column = jax.ShapeDtypeStruct((g, coarse), f32)
    spread_table = jax.ShapeDtypeStruct((2 * coarse, fine), bf16)
    return pl.pallas_call(
        functools.partial(prepare_body, block),
        out_shape=(
            jax.ShapeDtypeStruct((levels, g, 2 * depth), bf16),
            column,
            column,
            spread_table,
            spread_table,
        ),
        in_specs=[HBM] * 6,
        out_specs=[VMEM] * 5,
        scratch_shapes=[
            pltpu.VMEM((levels // block, g, block, feat), f32),
            pltpu.VMEM(bias.shape, f32),
            pltpu.VMEM(planck.shape, f32),
            pltpu.VMEM(share.shape, f32),
            pltpu.VMEM(stencil.shape, jnp.int32),
            pltpu.VMEM(weight.shape, f32),
            pltpu.SemaphoreType.DMA((5 + levels // block,)),
        ],
        compiler_params=pltpu.CompilerParams(vmem_limit_bytes=28 * MIB),
        cost_estimate=pl.CostEstimate(
            flops=10 * g * levels * feat, bytes_accessed=8 * g * levels * depth, transcendentals=0
        ),
        name="prepare",
    )(*(stay(x) for x in (absorb, bias, planck, share, stencil, weight)))


def trans_of(z):
    low = jnp.log(1.0 + jnp.exp(jnp.minimum(z, 40.0)))
    return jnp.exp(-0.1 * jnp.maximum(low, z))


def flux_body(block, scale, table, first, second, planck, share, out, other, right, zs, ts, downs, warms):
    levels, g, double = table.shape
    depth = double // 2
    feat = depth - levels
    half = first.shape[1]
    n = 2 * half
    blocks = levels // block
    for i, rows in enumerate((first, second)):
        lanes = slice(half * i, half * (i + 1))
        parts = split(rows[0:feat, :], 2)
        right[0:feat, lanes] = parts[0]
        right[depth : depth + feat, lanes] = parts[1]
        warms[0:levels, lanes] = 2.0 + jnp.tanh(rows[0:levels, :])
    right[feat:depth, :] = jnp.ones((levels, n), bf16)
    right[depth + feat : double, :] = jnp.zeros((levels, n), bf16)
    warms[levels : levels + 8, :] = jnp.zeros((8, n), f32)
    weight = jnp.concatenate([planck[...]] * 2, axis=1)

    def fold(x):
        return jnp.sum(x.reshape(g // 8, 8, n), axis=0)

    def absorb(b, slot):
        a = table[pl.ds(b * block, block)].reshape(block * g, double)
        c = right[0:depth, :]
        z = dot(a[:, 0:depth], c) + dot(a[:, depth:double], c)
        zs[slot] = z + dot(a[:, 0:depth], right[depth:double, :])

    def fall(b, slot, d):
        for j in range(block):
            l = b * block + j
            t = trans_of(zs[slot, j * g : (j + 1) * g, :])
            ts[l] = t
            d = t * d + weight * (warms[pl.ds(l, 1), :] - warms[pl.ds(l + 1, 1), :])
            downs[l + 1] = fold(d)
        return d

    lights = [rows[feat : feat + 1, :] for rows in (first, second)]
    d = jnp.concatenate([share[...]] * 2, axis=1) * jnp.concatenate(lights, axis=1)
    d = d - weight * warms[0:1, :]
    downs[0] = fold(d)
    absorb(0, 0)

    def step(i, d):
        absorb(2 * i + 1, 1)
        d = fall(2 * i, 0, d)
        absorb(jnp.minimum(2 * i + 2, blocks - 1), 0)
        return fall(2 * i + 1, 1, d)

    d = lax.fori_loop(0, blocks // 2, step, d)
    v = 0.3 * d

    def climb(i, carry):
        v, below = carry
        l = levels - 1 - i
        rise = warms[pl.ds(l, 1), :] - warms[pl.ds(jnp.maximum(l - 1, 0), 1), :]
        v = ts[l] * v + weight * rise
        above = fold(v)
        downs[l + 1] = (downs[l] - downs[l + 1]) + (below - above)
        return v, above

    lax.fori_loop(0, levels, climb, (v, fold(v)), unroll=8)
    heat = downs[1 : levels + 1, 0, :]
    for s in range(1, 8):
        heat = heat + downs[1 : levels + 1, s, :]
    here = warms[0:levels, :]
    prior = jnp.concatenate([here[0:1], here[0 : levels - 1]], axis=0)
    total = jnp.sum(fold(weight), axis=0, keepdims=True)
    heat = scale * (heat + total * ((here - warms[1 : levels + 1, :]) + (here - prior)))
    out[...] = heat[:, 0:half]
    other[...] = heat[:, half:n]


def flux(table, first, second, planck, share, scale):
    levels, g, double = table.shape
    half = first.shape[1]
    n = 2 * half
    block = 8
    heat = jax.ShapeDtypeStruct((levels, half), f32)
    return pl.pallas_call(
        functools.partial(flux_body, block, scale),
        out_shape=(heat, heat),
        in_specs=[VMEM] * 5,
        out_specs=[VMEM] * 2,
        scratch_shapes=[
            pltpu.VMEM((double, n), bf16),
            pltpu.VMEM((2, block * g, n), f32),
            pltpu.VMEM((levels, g, n), f32),
            pltpu.VMEM((levels + 1, 8, n), f32),
            pltpu.VMEM((levels + 8, n), f32),
        ],
        compiler_params=pltpu.CompilerParams(vmem_limit_bytes=20 * MIB),
        cost_estimate=pl.CostEstimate(
            flops=3 * g * levels * double * n,
            bytes_accessed=2 * g * levels * double,
            transcendentals=3 * g * levels * n,
        ),
        name="flux",
    )(table, first, second, planck, share)


def spread_body(own, first, second, parity, high, low, out):
    n = own.shape[1]
    lane = lax.broadcasted_iota(jnp.int32, own.shape, 1)
    late = jnp.where(lane >= n // 2, 1, 0)
    halo = jnp.where(late == parity[0], first[...], second[...])
    wide = jnp.concatenate([own[...], halo], axis=1)
    a, c = split(wide, 2)
    out[...] = dot(a, high[...]) + (dot(a, low[...]) + dot(c, high[...]))


def spread(own, first, second, parity, high, low):
    levels = own.shape[0]
    fine = high.shape[1]
    return pl.pallas_call(
        spread_body,
        out_shape=jax.ShapeDtypeStruct((levels, fine), f32),
        in_specs=[VMEM] * 3 + [pl.BlockSpec(memory_space=pltpu.SMEM)] + [VMEM] * 2,
        out_specs=VMEM,
        compiler_params=pltpu.CompilerParams(vmem_limit_bytes=16 * MIB),
        name="spread",
    )(own, first, second, parity, high, low)


def shards(
    state, cosine, grouping, sunlit, absorb, level_bias, planck, solar_share, stencil, stencil_weight
):
    fine, fields, levels = state.shape
    coarse = fine // 4
    n_sec = lax.axis_size("sec")
    devices = n_sec * lax.axis_size("col")
    columns = state.transpose(1, 2, 0).reshape(fields * levels, fine)
    rows = group(columns, cosine[None], grouping, sunlit)

    def swap(x, m):
        return lax.ppermute(x, "sec", [(i, i ^ m) for i in range(n_sec)])

    got = [rows] + [swap(rows, m) for m in range(1, n_sec)]
    table, weight, share, near, far = prepare(
        absorb, level_bias, planck[None], solar_share[None], stencil, stencil_weight, coarse
    )
    scale = 4.0 / (planck.shape[0] * n_sec)
    total, last = flux(table, got[0], got[1], weight, share, scale)
    returned = [swap(last, 1)]
    for m in range(2, n_sec, 2):
        *pair, total = lax.optimization_barrier((got[m], got[m + 1], total))
        heats = flux(table, *pair, weight, share, scale)
        returned += [swap(heats[0], m), swap(heats[1], m + 1)]
    for part in returned:
        total = total + part
    pairs = [(i, i ^ 1) for i in range(devices)]
    across = [(i, (i + 1) % devices if i % 2 else (i - 1) % devices) for i in range(devices)]
    second = lax.ppermute(total, ("sec", "col"), across)
    first = lax.ppermute(total, ("sec", "col"), pairs)
    parity = jnp.bitwise_and(lax.axis_index(("sec", "col")), 1).astype(jnp.int32).reshape(1)
    return spread(total, first, second, parity, near, far)


def solution(mesh):
    placed = (
        P(("sec", "col"), None, None),
        P(("sec", "col")),
        P(("sec", "col"), None),
        P(("sec", "col")),
        P("sec", None, None),
        P("sec", None),
        P("sec"),
        P("sec"),
        P(None, ("sec", "col")),
        P(None, ("sec", "col")),
    )
    return jax.shard_map(
        shards, mesh=mesh, in_specs=placed, out_specs=P(None, ("sec", "col")), check_vma=False
    )
```

```python
import functools

import jax
import jax.numpy as jnp
from jax import lax
from jax.experimental import pallas as pl
from jax.experimental.pallas import tpu as pltpu
from jax.sharding import PartitionSpec as P

RIM = 8
LOG2E = 1.4426950408889634
MIB = 1 << 20
bf16 = jnp.bfloat16
f32 = jnp.float32
VMEM = pl.BlockSpec(memory_space=pltpu.VMEM)


def split(x, parts):
    terms = []
    for _ in range(parts):
        term = x.astype(bf16)
        terms.append(term)
        x = x - term.astype(f32)
    return terms


def dot(a, b):
    return jnp.dot(a, b, preferred_element_type=f32)


HBM = pl.BlockSpec(memory_space=pltpu.HBM)


def stay(x):
    return pltpu.with_memory_space_constraint(x, pltpu.HBM)


def group_body(state_in, cosine_in, grouping_in, sunlit, out, state, cosine, grouping, sems):
    copies = [
        pltpu.make_async_copy(source, target, sems.at[i])
        for i, (source, target) in enumerate(
            ((grouping_in, grouping), (cosine_in, cosine), (state_in, state))
        )
    ]
    for copy in copies:
        copy.start()
    feat, fine = state.shape
    coarse = out.shape[1]
    place = lax.broadcasted_iota(jnp.int32, (fine, fine), 0)
    member = lax.broadcasted_iota(jnp.int32, (fine, coarse), 0) // 4
    home = lax.broadcasted_iota(jnp.int32, (fine, coarse), 1)
    mean = jnp.where(member == home, 0.25, 0.0).astype(bf16)
    copies[0].wait()
    picks = jnp.where(place == grouping[...], 1.0, 0.0).astype(bf16)
    weights = dot(picks, mean).astype(bf16)
    copies[1].wait()
    copies[2].wait()
    total = jnp.zeros((feat, coarse), f32)
    for term in split(state[...], 3)[::-1]:
        total = total + dot(term, weights)
    out[0:feat, :] = total
    light = jnp.zeros((8, coarse), f32)
    for term in split(jnp.broadcast_to(cosine[...], (8, fine)), 3)[::-1]:
        light = light + dot(term, weights)
    lane = lax.broadcasted_iota(jnp.int32, (8, coarse), 1)
    out[feat : feat + 8, :] = jnp.where(lane < sunlit[0], 4.0 * light, 0.0)


def group(state, cosine, grouping, sunlit):
    feat, fine = state.shape
    coarse = fine // 4
    return pl.pallas_call(
        group_body,
        out_shape=jax.ShapeDtypeStruct((feat + 8, coarse), f32),
        in_specs=[HBM, HBM, HBM, pl.BlockSpec(memory_space=pltpu.SMEM)],
        out_specs=VMEM,
        scratch_shapes=[
            pltpu.VMEM((feat, fine), f32),
            pltpu.VMEM((1, fine), f32),
            pltpu.VMEM((1, fine), jnp.int32),
            pltpu.SemaphoreType.DMA((3,)),
        ],
        compiler_params=pltpu.CompilerParams(vmem_limit_bytes=16 * MIB),
        cost_estimate=pl.CostEstimate(
            flops=8 * feat * fine * coarse, bytes_accessed=4 * feat * fine, transcendentals=0
        ),
        name="group",
    )(stay(state), stay(cosine), stay(grouping), sunlit)


def prepare_body(
    block,
    absorb_in,
    bias_in,
    planck_in,
    share_in,
    stencil_in,
    weight_in,
    table,
    planck_out,
    share_out,
    high,
    low,
    absorb,
    bias,
    planck,
    share,
    stencil,
    weight,
    sems,
):
    levels, g, double = table.shape
    depth = double // 2
    blocks = levels // block
    small = [
        pltpu.make_async_copy(source, target, sems.at[i])
        for i, (source, target) in enumerate(
            (
                (bias_in, bias),
                (planck_in, planck),
                (share_in, share),
                (stencil_in, stencil),
                (weight_in, weight),
            )
        )
    ]
    large = [
        pltpu.make_async_copy(
            absorb_in.at[:, pl.ds(i * block, block), :], absorb.at[i], sems.at[len(small) + i]
        )
        for i in range(blocks)
    ]
    for copy in small + large:
        copy.start()
    for copy in small:
        copy.wait()

    def column(row):
        n = row.shape[1]
        eye = lax.broadcasted_iota(jnp.int32, (n, n), 0) == lax.broadcasted_iota(
            jnp.int32, (n, n), 1
        )
        return jnp.sum(jnp.where(eye, row, 0.0), axis=1, keepdims=True)

    planck_out[...] = jnp.broadcast_to(column(planck[...]), planck_out.shape)
    share_out[...] = jnp.broadcast_to(column(share[...]), share_out.shape)
    wide, fine = high.shape
    place = lax.broadcasted_iota(jnp.int32, (wide, fine), 0)
    total = jnp.zeros((wide, fine), f32)
    for k in range(stencil.shape[0]):
        at = stencil[k : k + 1, :]
        spot = jnp.where(at < RIM, wide - RIM + at, at - RIM)
        total = total + jnp.where(place == spot, weight[k : k + 1, :], 0.0)
    parts = split(total, 2)
    high[...] = parts[0]
    low[...] = parts[1]

    b = bias[...] * LOG2E
    lane = lax.broadcasted_iota(jnp.int32, b.shape, 1)
    for i in range(blocks):
        large[i].wait()
        for j in range(block):
            tail = jnp.where(lane == i * block + j, b, 0.0)
            parts = split(jnp.concatenate([absorb[i, :, j, :], tail], axis=1), 2)
            table[i * block + j, :, 0:depth] = parts[0]
            table[i * block + j, :, depth:double] = parts[1]


def prepare(absorb, bias, planck, share, stencil, weight, coarse):
    g, levels, feat = absorb.shape
    fine = stencil.shape[1]
    block = 8
    depth = feat + levels
    column = jax.ShapeDtypeStruct((g, coarse), f32)
    spread_table = jax.ShapeDtypeStruct((2 * coarse, fine), bf16)
    return pl.pallas_call(
        functools.partial(prepare_body, block),
        out_shape=(
            jax.ShapeDtypeStruct((levels, g, 2 * depth), bf16),
            column,
            column,
            spread_table,
            spread_table,
        ),
        in_specs=[HBM] * 6,
        out_specs=[VMEM] * 5,
        scratch_shapes=[
            pltpu.VMEM((levels // block, g, block, feat), f32),
            pltpu.VMEM(bias.shape, f32),
            pltpu.VMEM(planck.shape, f32),
            pltpu.VMEM(share.shape, f32),
            pltpu.VMEM(stencil.shape, jnp.int32),
            pltpu.VMEM(weight.shape, f32),
            pltpu.SemaphoreType.DMA((5 + levels // block,)),
        ],
        compiler_params=pltpu.CompilerParams(vmem_limit_bytes=28 * MIB),
        cost_estimate=pl.CostEstimate(
            flops=10 * g * levels * feat, bytes_accessed=8 * g * levels * depth, transcendentals=0
        ),
        name="prepare",
    )(*(stay(x) for x in (absorb, bias, planck, share, stencil, weight)))


def trans_of(y):
    low = lax.log2(1.0 + jnp.exp2(jnp.minimum(y, 64.0)))
    return jnp.exp2(-0.1 * jnp.maximum(low, y))


def flux_body(block, scale, table, first, second, planck, share, out, other, right, zs, ts, downs, warms):
    levels, g, double = table.shape
    depth = double // 2
    feat = depth - levels
    half = first.shape[1]
    n = 2 * half
    blocks = levels // block
    for i, rows in enumerate((first, second)):
        lanes = slice(half * i, half * (i + 1))
        parts = split(rows[0:feat, :] * LOG2E, 2)
        right[0:feat, lanes] = parts[0]
        right[depth : depth + feat, lanes] = parts[1]
        warms[0:levels, lanes] = 2.0 + jnp.tanh(rows[0:levels, :])
    right[feat:depth, :] = jnp.ones((levels, n), bf16)
    right[depth + feat : double, :] = jnp.zeros((levels, n), bf16)
    warms[levels : levels + 8, :] = jnp.zeros((8, n), f32)
    weight = jnp.concatenate([planck[...]] * 2, axis=1)

    def fold(x):
        return jnp.sum(x.reshape(g // 8, 8, n), axis=0)

    def absorb(b, slot):
        a = table[pl.ds(b * block, block)].reshape(block * g, double)
        c = right[0:depth, :]
        z = dot(a[:, 0:depth], c) + dot(a[:, depth:double], c)
        zs[slot] = z + dot(a[:, 0:depth], right[depth:double, :])

    def fall(b, slot, d):
        for j in range(block):
            l = b * block + j
            t = trans_of(zs[slot, j * g : (j + 1) * g, :])
            ts[l] = t
            d = t * d + weight * (warms[pl.ds(l, 1), :] - warms[pl.ds(l + 1, 1), :])
            downs[l + 1] = fold(d)
        return d

    lights = [rows[feat : feat + 1, :] for rows in (first, second)]
    d = jnp.concatenate([share[...]] * 2, axis=1) * jnp.concatenate(lights, axis=1)
    d = d - weight * warms[0:1, :]
    downs[0] = fold(d)
    absorb(0, 0)

    for b in range(blocks):
        if b + 1 < blocks:
            absorb(b + 1, (b + 1) % 2)
        d = fall(b, b % 2, d)
    v = 0.3 * d

    def climb(i, carry):
        v, below = carry
        l = levels - 1 - i
        rise = warms[pl.ds(l, 1), :] - warms[pl.ds(jnp.maximum(l - 1, 0), 1), :]
        v = ts[l] * v + weight * rise
        above = fold(v)
        downs[l + 1] = (downs[l] - downs[l + 1]) + (below - above)
        return v, above

    lax.fori_loop(0, levels, climb, (v, fold(v)), unroll=8)
    heat = downs[1 : levels + 1, 0, :]
    for s in range(1, 8):
        heat = heat + downs[1 : levels + 1, s, :]
    here = warms[0:levels, :]
    prior = jnp.concatenate([here[0:1], here[0 : levels - 1]], axis=0)
    total = jnp.sum(fold(weight), axis=0, keepdims=True)
    heat = scale * (heat + total * ((here - warms[1 : levels + 1, :]) + (here - prior)))
    out[...] = heat[:, 0:half]
    other[...] = heat[:, half:n]


def flux(table, first, second, planck, share, scale):
    levels, g, double = table.shape
    half = first.shape[1]
    n = 2 * half
    block = 4
    heat = jax.ShapeDtypeStruct((levels, half), f32)
    return pl.pallas_call(
        functools.partial(flux_body, block, scale),
        out_shape=(heat, heat),
        in_specs=[VMEM] * 5,
        out_specs=[VMEM] * 2,
        scratch_shapes=[
            pltpu.VMEM((double, n), bf16),
            pltpu.VMEM((2, block * g, n), f32),
            pltpu.VMEM((levels, g, n), f32),
            pltpu.VMEM((levels + 1, 8, n), f32),
            pltpu.VMEM((levels + 8, n), f32),
        ],
        compiler_params=pltpu.CompilerParams(vmem_limit_bytes=20 * MIB),
        cost_estimate=pl.CostEstimate(
            flops=3 * g * levels * double * n,
            bytes_accessed=2 * g * levels * double,
            transcendentals=3 * g * levels * n,
        ),
        name="flux",
    )(table, first, second, planck, share)


def spread_body(own, first, second, parity, high, low, out):
    n = own.shape[1]
    lane = lax.broadcasted_iota(jnp.int32, own.shape, 1)
    late = jnp.where(lane >= n // 2, 1, 0)
    halo = jnp.where(late == parity[0], first[...], second[...])
    wide = jnp.concatenate([own[...], halo], axis=1)
    a, c = split(wide, 2)
    out[...] = dot(a, high[...]) + (dot(a, low[...]) + dot(c, high[...]))


def spread(own, first, second, parity, high, low):
    levels = own.shape[0]
    fine = high.shape[1]
    return pl.pallas_call(
        spread_body,
        out_shape=jax.ShapeDtypeStruct((levels, fine), f32),
        in_specs=[VMEM] * 3 + [pl.BlockSpec(memory_space=pltpu.SMEM)] + [VMEM] * 2,
        out_specs=VMEM,
        compiler_params=pltpu.CompilerParams(vmem_limit_bytes=16 * MIB),
        name="spread",
    )(own, first, second, parity, high, low)


def shards(
    state, cosine, grouping, sunlit, absorb, level_bias, planck, solar_share, stencil, stencil_weight
):
    fine, fields, levels = state.shape
    coarse = fine // 4
    n_sec = lax.axis_size("sec")
    devices = n_sec * lax.axis_size("col")
    columns = state.transpose(1, 2, 0).reshape(fields * levels, fine)
    rows = group(columns, cosine[None], grouping, sunlit)

    def swap(x, m):
        return lax.ppermute(x, "sec", [(i, i ^ m) for i in range(n_sec)])

    table, weight, share, near, far = prepare(
        absorb, level_bias, planck[None], solar_share[None], stencil, stencil_weight, coarse
    )
    scale = 4.0 / (planck.shape[0] * n_sec)
    got = [rows] + [swap(rows, m) for m in range(1, n_sec - 1)]
    later, table = lax.optimization_barrier((rows, table))
    got.append(swap(later, n_sec - 1))
    total, last = flux(table, got[0], got[1], weight, share, scale)
    returned = [swap(last, 1)]
    for m in range(2, n_sec, 2):
        *pair, total = lax.optimization_barrier((got[m], got[m + 1], total))
        heats = flux(table, *pair, weight, share, scale)
        returned += [swap(heats[0], m), swap(heats[1], m + 1)]
    for part in returned:
        total = total + part
    pairs = [(i, i ^ 1) for i in range(devices)]
    across = [(i, (i + 1) % devices if i % 2 else (i - 1) % devices) for i in range(devices)]
    second = lax.ppermute(total, ("sec", "col"), across)
    first = lax.ppermute(total, ("sec", "col"), pairs)
    parity = jnp.bitwise_and(lax.axis_index(("sec", "col")), 1).astype(jnp.int32).reshape(1)
    return spread(total, second, first, 1 - parity, near, far)


def solution(mesh):
    placed = (
        P(("sec", "col"), None, None),
        P(("sec", "col")),
        P(("sec", "col"), None),
        P(("sec", "col")),
        P("sec", None, None),
        P("sec", None),
        P("sec"),
        P("sec"),
        P(None, ("sec", "col")),
        P(None, ("sec", "col")),
    )
    return jax.shard_map(
        shards, mesh=mesh, in_specs=placed, out_specs=P(None, ("sec", "col")), check_vma=False
    )
```

```python
import functools

import jax
import jax.numpy as jnp
from jax import lax
from jax.experimental import pallas as pl
from jax.experimental.pallas import tpu as pltpu
from jax.sharding import PartitionSpec as P

RIM = 8
LOG2E = 1.4426950408889634
MIB = 1 << 20
bf16 = jnp.bfloat16
f32 = jnp.float32
VMEM = pl.BlockSpec(memory_space=pltpu.VMEM)


def split(x, parts):
    terms = []
    for _ in range(parts):
        term = x.astype(bf16)
        terms.append(term)
        x = x - term.astype(f32)
    return terms


def dot(a, b):
    return jnp.dot(a, b, preferred_element_type=f32)


HBM = pl.BlockSpec(memory_space=pltpu.HBM)


def stay(x):
    return pltpu.with_memory_space_constraint(x, pltpu.HBM)


def column_of(place, coarse):
    quarter = coarse // 4
    inner = jnp.where(place < 2 * quarter, place + 2 * quarter, place - quarter)
    return jnp.where(place < quarter, place, inner)


def group_body(state_in, cosine_in, grouping_in, sunlit, out, state, cosine, grouping, sems):
    copies = [
        pltpu.make_async_copy(source, target, sems.at[i])
        for i, (source, target) in enumerate(
            ((grouping_in, grouping), (cosine_in, cosine), (state_in, state))
        )
    ]
    for copy in copies:
        copy.start()
    feat, fine = state.shape
    coarse = out.shape[1]
    place = lax.broadcasted_iota(jnp.int32, (fine, fine), 0)
    member = lax.broadcasted_iota(jnp.int32, (fine, coarse), 0) // 4
    home = column_of(lax.broadcasted_iota(jnp.int32, (fine, coarse), 1), coarse)
    mean = jnp.where(member == home, 0.25, 0.0).astype(bf16)
    copies[0].wait()
    picks = jnp.where(place == grouping[...], 1.0, 0.0).astype(bf16)
    weights = dot(picks, mean).astype(bf16)
    copies[1].wait()
    copies[2].wait()
    total = jnp.zeros((feat, coarse), f32)
    for term in split(state[...], 3)[::-1]:
        total = total + dot(term, weights)
    out[0:feat, :] = total
    light = jnp.zeros((8, coarse), f32)
    for term in split(jnp.broadcast_to(cosine[...], (8, fine)), 3)[::-1]:
        light = light + dot(term, weights)
    lane = column_of(lax.broadcasted_iota(jnp.int32, (8, coarse), 1), coarse)
    out[feat : feat + 8, :] = jnp.where(lane < sunlit[0], 4.0 * light, 0.0)


def group(state, cosine, grouping, sunlit):
    feat, fine = state.shape
    coarse = fine // 4
    return pl.pallas_call(
        group_body,
        out_shape=jax.ShapeDtypeStruct((feat + 8, coarse), f32),
        in_specs=[HBM, HBM, HBM, pl.BlockSpec(memory_space=pltpu.SMEM)],
        out_specs=VMEM,
        scratch_shapes=[
            pltpu.VMEM((feat, fine), f32),
            pltpu.VMEM((1, fine), f32),
            pltpu.VMEM((1, fine), jnp.int32),
            pltpu.SemaphoreType.DMA((3,)),
        ],
        compiler_params=pltpu.CompilerParams(vmem_limit_bytes=16 * MIB),
        cost_estimate=pl.CostEstimate(
            flops=8 * feat * fine * coarse, bytes_accessed=4 * feat * fine, transcendentals=0
        ),
        name="group",
    )(stay(state), stay(cosine), stay(grouping), sunlit)


def trans_of(y):
    low = lax.log2(1.0 + jnp.exp2(jnp.minimum(y, 64.0)))
    return jnp.exp2(-0.1 * jnp.maximum(low, y))


def sweeps(block, scale, table, chunks, planck, share, outs, scratch):
    right, zs, ts, downs, warms = scratch
    levels, g, double = table.shape
    depth = double // 2
    feat = depth - levels
    half = chunks[0].shape[1]
    count = len(chunks)
    n = count * half
    blocks = levels // block
    top = 0 if count == 1 else depth
    for i, rows in enumerate(chunks):
        lanes = slice(half * i, half * (i + 1))
        under = slice(half, 2 * half) if count == 1 else lanes
        parts = split(rows[0:feat, :] * LOG2E, 2)
        right[0:feat, lanes] = parts[0]
        right[top : top + feat, under] = parts[1]
        warms[0:levels, lanes] = 2.0 + jnp.tanh(rows[0:levels, :])
        right[feat:depth, lanes] = jnp.ones((levels, half), bf16)
        right[top + feat : top + depth, under] = jnp.zeros((levels, half), bf16)
    warms[levels : levels + 8, :] = jnp.zeros((8, n), f32)

    def fold(x):
        return jnp.sum(x.reshape(g // 8, 8, n), axis=0)

    def absorb(b):
        a = table[b * block : (b + 1) * block].reshape(block * g, double)
        c = right[0:depth, :]
        z = dot(a[:, 0:depth], c) + dot(a[:, depth:double], c)
        if count == 1:
            zs[b % 2] = z[:, 0:n] + z[:, n : 2 * n]
        else:
            zs[b % 2] = z + dot(a[:, 0:depth], right[depth:double, :])

    absorb(0)
    weight = jnp.concatenate([planck[...]] * count, axis=1)
    lights = jnp.concatenate([rows[feat : feat + 1, :] for rows in chunks], axis=1)
    d = jnp.concatenate([share[...]] * count, axis=1) * lights - weight * warms[0:1, :]
    downs[0] = fold(d)
    for b in range(blocks):
        if b + 1 < blocks:
            absorb(b + 1)
        for j in range(block):
            l = b * block + j
            t = trans_of(zs[b % 2, j * g : (j + 1) * g, :])
            ts[l] = t
            d = t * d + weight * (warms[l : l + 1, :] - warms[l + 1 : l + 2, :])
            downs[l + 1] = fold(d)
    v = 0.3 * d

    def climb(i, carry):
        v, below = carry
        l = levels - 1 - i
        rise = warms[pl.ds(l, 1), :] - warms[pl.ds(jnp.maximum(l - 1, 0), 1), :]
        v = ts[l] * v + weight * rise
        above = fold(v)
        downs[l + 1] = (downs[l] - downs[l + 1]) + (below - above)
        return v, above

    lax.fori_loop(0, levels, climb, (v, fold(v)), unroll=8)
    heat = downs[1 : levels + 1, 0, :]
    for s in range(1, 8):
        heat = heat + downs[1 : levels + 1, s, :]
    here = warms[0:levels, :]
    prior = jnp.concatenate([here[0:1], here[0 : levels - 1]], axis=0)
    total = jnp.sum(fold(weight), axis=0, keepdims=True)
    heat = scale * (heat + total * ((here - warms[1 : levels + 1, :]) + (here - prior)))
    wide = n // len(outs)
    for i, out in enumerate(outs):
        out[...] = heat[:, wide * i : wide * (i + 1)]


def sweep_scratch(block, g, levels, depth, count, half):
    n = count * half
    return [
        pltpu.VMEM((depth, 2 * n) if count == 1 else (2 * depth, n), bf16),
        pltpu.VMEM((2, block * g, n), f32),
        pltpu.VMEM((levels, g, n), f32),
        pltpu.VMEM((levels + 1, 8, n), f32),
        pltpu.VMEM((levels + 8, n), f32),
    ]


def prepare_body(
    block,
    absorb_in,
    bias_in,
    planck_in,
    share_in,
    stencil_in,
    weight_in,
    table,
    planck_out,
    share_out,
    high,
    low,
    absorb,
    bias,
    planck,
    share,
    stencil,
    weight,
    sems,
):
    levels, g, double = table.shape
    depth = double // 2
    blocks = levels // block
    small = [
        pltpu.make_async_copy(source, target, sems.at[i])
        for i, (source, target) in enumerate(
            (
                (bias_in, bias),
                (planck_in, planck),
                (share_in, share),
                (stencil_in, stencil),
                (weight_in, weight),
            )
        )
    ]
    large = [
        pltpu.make_async_copy(
            absorb_in.at[:, pl.ds(i * block, block), :], absorb.at[i], sems.at[len(small) + i]
        )
        for i in range(blocks)
    ]
    for copy in small + large:
        copy.start()
    for copy in small:
        copy.wait()

    def column(row):
        n = row.shape[1]
        eye = lax.broadcasted_iota(jnp.int32, (n, n), 0) == lax.broadcasted_iota(
            jnp.int32, (n, n), 1
        )
        return jnp.sum(jnp.where(eye, row, 0.0), axis=1, keepdims=True)

    planck_out[...] = jnp.broadcast_to(column(planck[...]), planck_out.shape)
    share_out[...] = jnp.broadcast_to(column(share[...]), share_out.shape)
    wide, fine = high.shape
    quarter = wide // 6
    place = lax.broadcasted_iota(jnp.int32, (wide, fine), 0)
    total = jnp.zeros((wide, fine), f32)
    for k in range(stencil.shape[0]):
        at = stencil[k : k + 1, :]
        own = at - RIM
        spot = jnp.where(own < 3 * quarter, own + quarter, own - 2 * quarter)
        spot = jnp.where(own < quarter, own, spot)
        spot = jnp.where(own < 0, wide + own, spot)
        spot = jnp.where(own < 4 * quarter, spot, own)
        total = total + jnp.where(place == spot, weight[k : k + 1, :], 0.0)
    parts = split(total, 2)
    high[...] = parts[0]
    low[...] = parts[1]

    b = bias[...] * LOG2E
    lane = lax.broadcasted_iota(jnp.int32, b.shape, 1)
    for i in range(blocks):
        large[i].wait()
        for j in range(block):
            tail = jnp.where(lane == i * block + j, b, 0.0)
            parts = split(jnp.concatenate([absorb[i, :, j, :], tail], axis=1), 2)
            table[i * block + j, :, 0:depth] = parts[0]
            table[i * block + j, :, depth:double] = parts[1]


def prepare(absorb, bias, planck, share, stencil, weight, coarse):
    g, levels, feat = absorb.shape
    fine = stencil.shape[1]
    block = 8
    depth = feat + levels
    column = jax.ShapeDtypeStruct((g, coarse), f32)
    spread_table = jax.ShapeDtypeStruct((3 * coarse // 2, fine), bf16)
    return pl.pallas_call(
        functools.partial(prepare_body, block),
        out_shape=(
            jax.ShapeDtypeStruct((levels, g, 2 * depth), bf16),
            column,
            column,
            spread_table,
            spread_table,
        ),
        in_specs=[HBM] * 6,
        out_specs=[VMEM] * 5,
        scratch_shapes=[
            pltpu.VMEM((levels // block, g, block, feat), f32),
            pltpu.VMEM(bias.shape, f32),
            pltpu.VMEM(planck.shape, f32),
            pltpu.VMEM(share.shape, f32),
            pltpu.VMEM(stencil.shape, jnp.int32),
            pltpu.VMEM(weight.shape, f32),
            pltpu.SemaphoreType.DMA((5 + levels // block,)),
        ],
        compiler_params=pltpu.CompilerParams(vmem_limit_bytes=28 * MIB),
        cost_estimate=pl.CostEstimate(
            flops=10 * g * levels * feat, bytes_accessed=8 * g * levels * depth, transcendentals=0
        ),
        name="prepare",
    )(*(stay(x) for x in (absorb, bias, planck, share, stencil, weight)))


def flux_body(block, scale, part, table, planck, share, first, second, out, other, *scratch):
    chunks = [first, second]
    if part is not None:
        joined, *scratch = scratch
        half = joined.shape[1] // 2
        for i, rows in enumerate(chunks):
            joined[:, half * i : half * (i + 1)] = rows[:, half * part : half * (part + 1)]
        chunks = [joined]
    sweeps(block, scale, table, chunks, planck, share, [out, other], scratch)


def flux(table, planck, share, first, second, scale, part=None):
    levels, g, double = table.shape
    width = first.shape[1]
    count = 2 if part is None else 1
    block = 4
    heat = jax.ShapeDtypeStruct((levels, width * count // 2), f32)
    joined = [] if part is None else [pltpu.VMEM(first.shape, f32)]
    return pl.pallas_call(
        functools.partial(flux_body, block, scale, part),
        out_shape=(heat, heat),
        in_specs=[VMEM] * 5,
        out_specs=(VMEM, VMEM),
        scratch_shapes=joined + sweep_scratch(block, g, levels, double // 2, count, width),
        compiler_params=pltpu.CompilerParams(vmem_limit_bytes=20 * MIB),
        cost_estimate=pl.CostEstimate(
            flops=3 * g * levels * double * count * width,
            bytes_accessed=2 * g * levels * double,
            transcendentals=3 * g * levels * count * width,
        ),
        name="flux",
    )(table, planck, share, first, second)


def spread_body(first, second, side, far, own, back, ends, parity, high, low, out):
    n = ends.shape[1]
    lane = lax.broadcasted_iota(jnp.int32, ends.shape, 1)
    late = jnp.where(lane >= n // 2, 1, 0)
    halo = jnp.where(late == parity[0], first[...], second[...])
    middle = own[:, n : 2 * n] + back[:, n : 2 * n] + side[...] + far[...]
    wide = jnp.concatenate([ends[...], middle, halo], axis=1)
    a, c = split(wide, 2)
    out[...] = dot(a, high[...]) + (dot(a, low[...]) + dot(c, high[...]))


def spread(first, second, side, far, own, back, ends, parity, high, low):
    levels = ends.shape[0]
    fine = high.shape[1]
    return pl.pallas_call(
        spread_body,
        out_shape=jax.ShapeDtypeStruct((levels, fine), f32),
        in_specs=[VMEM] * 7 + [pl.BlockSpec(memory_space=pltpu.SMEM)] + [VMEM] * 2,
        out_specs=VMEM,
        compiler_params=pltpu.CompilerParams(vmem_limit_bytes=16 * MIB),
        name="spread",
    )(first, second, side, far, own, back, ends, parity, high, low)


def shards(
    state, cosine, grouping, sunlit, absorb, level_bias, planck, solar_share, stencil, stencil_weight
):
    fine, fields, levels = state.shape
    coarse = fine // 4
    n_sec = lax.axis_size("sec")
    devices = n_sec * lax.axis_size("col")
    columns = state.transpose(1, 2, 0).reshape(fields * levels, fine)
    rows = group(columns, cosine[None], grouping, sunlit)

    def swap(x, m):
        return lax.ppermute(x, "sec", [(i, i ^ m) for i in range(n_sec)])

    scale = 4.0 / (planck.shape[0] * n_sec)
    got = [rows, swap(rows, 1), swap(rows, 2)]
    table, weight, share, near, far = prepare(
        absorb, level_bias, planck[None], solar_share[None], stencil, stencil_weight, coarse
    )
    later, table = lax.optimization_barrier((rows, table))
    got.append(swap(later, 3))
    own, heat = flux(table, weight, share, got[0], got[1], scale)
    *late, own, table = lax.optimization_barrier((*got[2:], own, table))
    back = swap(heat, 1)
    half = coarse // 2
    heats = flux(table, weight, share, *late, scale, 0)
    *late, table, h0, h1 = lax.optimization_barrier((*late, table, *heats))
    rest = flux(table, weight, share, *late, scale, 1)
    ends = own[:, :half] + back[:, :half] + swap(h0, 2) + swap(h1, 3)
    ends, *rest = lax.optimization_barrier((ends, *rest))
    side, diagonal = swap(rest[0], 2), swap(rest[1], 3)
    pairs = [(i, i ^ 1) for i in range(devices)]
    across = [(i, (i + 1) % devices if i % 2 else (i - 1) % devices) for i in range(devices)]
    second = lax.ppermute(ends, ("sec", "col"), across)
    first = lax.ppermute(ends, ("sec", "col"), pairs)
    parity = jnp.bitwise_and(lax.axis_index(("sec", "col")), 1).astype(jnp.int32).reshape(1)
    return spread(second, first, side, diagonal, own, back, ends, 1 - parity, near, far)


def solution(mesh):
    placed = (
        P(("sec", "col"), None, None),
        P(("sec", "col")),
        P(("sec", "col"), None),
        P(("sec", "col")),
        P("sec", None, None),
        P("sec", None),
        P("sec"),
        P("sec"),
        P(None, ("sec", "col")),
        P(None, ("sec", "col")),
    )
    return jax.shard_map(
        shards, mesh=mesh, in_specs=placed, out_specs=P(None, ("sec", "col")), check_vma=False
    )
```

```python
import functools

import jax
import jax.numpy as jnp
from jax import lax
from jax.experimental import pallas as pl
from jax.experimental.pallas import tpu as pltpu
from jax.sharding import PartitionSpec as P

RIM = 8
LOG2E = 1.4426950408889634
MIB = 1 << 20
bf16 = jnp.bfloat16
f32 = jnp.float32
VMEM = pl.BlockSpec(memory_space=pltpu.VMEM)


def split(x, parts):
    terms = []
    for _ in range(parts):
        term = x.astype(bf16)
        terms.append(term)
        x = x - term.astype(f32)
    return terms


def dot(a, b):
    return jnp.dot(a, b, preferred_element_type=f32)


HBM = pl.BlockSpec(memory_space=pltpu.HBM)


def stay(x):
    return pltpu.with_memory_space_constraint(x, pltpu.HBM)


def group_body(state_in, cosine_in, grouping_in, sunlit, out, state, cosine, grouping, sems):
    copies = [
        pltpu.make_async_copy(source, target, sems.at[i])
        for i, (source, target) in enumerate(
            ((grouping_in, grouping), (cosine_in, cosine), (state_in, state))
        )
    ]
    for copy in copies:
        copy.start()
    feat, fine = state.shape
    coarse = out.shape[1]
    place = lax.broadcasted_iota(jnp.int32, (fine, fine), 0)
    member = lax.broadcasted_iota(jnp.int32, (fine, coarse), 0) // 4
    home = lax.broadcasted_iota(jnp.int32, (fine, coarse), 1)
    mean = jnp.where(member == home, 0.25, 0.0).astype(bf16)
    copies[0].wait()
    picks = jnp.where(place == grouping[...], 1.0, 0.0).astype(bf16)
    weights = dot(picks, mean).astype(bf16)
    copies[1].wait()
    copies[2].wait()
    total = jnp.zeros((feat, coarse), f32)
    for term in split(state[...], 3)[::-1]:
        total = total + dot(term, weights)
    out[0:feat, :] = total
    light = jnp.zeros((8, coarse), f32)
    for term in split(jnp.broadcast_to(cosine[...], (8, fine)), 3)[::-1]:
        light = light + dot(term, weights)
    lane = lax.broadcasted_iota(jnp.int32, (8, coarse), 1)
    out[feat : feat + 8, :] = jnp.where(lane < sunlit[0], 4.0 * light, 0.0)


def group(state, cosine, grouping, sunlit):
    feat, fine = state.shape
    coarse = fine // 4
    return pl.pallas_call(
        group_body,
        out_shape=jax.ShapeDtypeStruct((feat + 8, coarse), f32),
        in_specs=[HBM, HBM, HBM, pl.BlockSpec(memory_space=pltpu.SMEM)],
        out_specs=VMEM,
        scratch_shapes=[
            pltpu.VMEM((feat, fine), f32),
            pltpu.VMEM((1, fine), f32),
            pltpu.VMEM((1, fine), jnp.int32),
            pltpu.SemaphoreType.DMA((3,)),
        ],
        compiler_params=pltpu.CompilerParams(vmem_limit_bytes=16 * MIB),
        cost_estimate=pl.CostEstimate(
            flops=8 * feat * fine * coarse, bytes_accessed=4 * feat * fine, transcendentals=0
        ),
        name="group",
    )(stay(state), stay(cosine), stay(grouping), sunlit)


def trans_of(y):
    low = lax.log2(1.0 + jnp.exp2(jnp.minimum(y, 64.0)))
    return jnp.exp2(-0.1 * jnp.maximum(low, y))


def sweeps(block, scale, table, chunks, planck, share, outs, scratch):
    right, zs, ts, downs, warms = scratch
    levels, g, double = table.shape
    depth = double // 2
    feat = depth - levels
    half = chunks[0].shape[1]
    count = len(chunks)
    n = count * half
    blocks = levels // block
    top = 0 if count == 1 else depth
    for i, rows in enumerate(chunks):
        lanes = slice(half * i, half * (i + 1))
        under = slice(half, 2 * half) if count == 1 else lanes
        parts = split(rows[0:feat, :] * LOG2E, 2)
        right[0:feat, lanes] = parts[0]
        right[top : top + feat, under] = parts[1]
        warms[0:levels, lanes] = 2.0 + jnp.tanh(rows[0:levels, :])
        right[feat:depth, lanes] = jnp.ones((levels, half), bf16)
        right[top + feat : top + depth, under] = jnp.zeros((levels, half), bf16)
    warms[levels : levels + 8, :] = jnp.zeros((8, n), f32)

    def fold(x):
        return jnp.sum(x.reshape(g // 8, 8, n), axis=0)

    def absorb(b):
        a = table[b * block : (b + 1) * block].reshape(block * g, double)
        c = right[0:depth, :]
        z = dot(a[:, 0:depth], c) + dot(a[:, depth:double], c)
        if count == 1:
            zs[b % 2] = z[:, 0:n] + z[:, n : 2 * n]
        else:
            zs[b % 2] = z + dot(a[:, 0:depth], right[depth:double, :])

    absorb(0)
    weight = jnp.concatenate([planck[...]] * count, axis=1)
    lights = jnp.concatenate([rows[feat : feat + 1, :] for rows in chunks], axis=1)
    d = jnp.concatenate([share[...]] * count, axis=1) * lights - weight * warms[0:1, :]
    downs[0] = fold(d)
    for b in range(blocks):
        if b + 1 < blocks:
            absorb(b + 1)
        for j in range(block):
            l = b * block + j
            t = trans_of(zs[b % 2, j * g : (j + 1) * g, :])
            ts[l] = t
            d = t * d + weight * (warms[l : l + 1, :] - warms[l + 1 : l + 2, :])
            downs[l + 1] = fold(d)
    v = 0.3 * d

    def climb(i, carry):
        v, below = carry
        l = levels - 1 - i
        rise = warms[pl.ds(l, 1), :] - warms[pl.ds(jnp.maximum(l - 1, 0), 1), :]
        v = ts[l] * v + weight * rise
        above = fold(v)
        downs[l + 1] = (downs[l] - downs[l + 1]) + (below - above)
        return v, above

    lax.fori_loop(0, levels, climb, (v, fold(v)), unroll=8)
    heat = downs[1 : levels + 1, 0, :]
    for s in range(1, 8):
        heat = heat + downs[1 : levels + 1, s, :]
    here = warms[0:levels, :]
    prior = jnp.concatenate([here[0:1], here[0 : levels - 1]], axis=0)
    total = jnp.sum(fold(weight), axis=0, keepdims=True)
    heat = scale * (heat + total * ((here - warms[1 : levels + 1, :]) + (here - prior)))
    for i, out in enumerate(outs):
        out[...] = heat[:, half * i : half * (i + 1)]


def sweep_scratch(block, g, levels, depth, count, half):
    n = count * half
    return [
        pltpu.VMEM((depth, 2 * n) if count == 1 else (2 * depth, n), bf16),
        pltpu.VMEM((2, block * g, n), f32),
        pltpu.VMEM((levels, g, n), f32),
        pltpu.VMEM((levels + 1, 8, n), f32),
        pltpu.VMEM((levels + 8, n), f32),
    ]


def prepare_body(
    block,
    absorb_in,
    bias_in,
    planck_in,
    share_in,
    stencil_in,
    weight_in,
    table,
    planck_out,
    share_out,
    high,
    low,
    absorb,
    bias,
    planck,
    share,
    stencil,
    weight,
    sems,
):
    levels, g, double = table.shape
    depth = double // 2
    blocks = levels // block
    small = [
        pltpu.make_async_copy(source, target, sems.at[i])
        for i, (source, target) in enumerate(
            (
                (bias_in, bias),
                (planck_in, planck),
                (share_in, share),
                (stencil_in, stencil),
                (weight_in, weight),
            )
        )
    ]
    large = [
        pltpu.make_async_copy(
            absorb_in.at[:, pl.ds(i * block, block), :], absorb.at[i], sems.at[len(small) + i]
        )
        for i in range(blocks)
    ]
    for copy in small + large:
        copy.start()
    for copy in small:
        copy.wait()

    def column(row):
        n = row.shape[1]
        eye = lax.broadcasted_iota(jnp.int32, (n, n), 0) == lax.broadcasted_iota(
            jnp.int32, (n, n), 1
        )
        return jnp.sum(jnp.where(eye, row, 0.0), axis=1, keepdims=True)

    planck_out[...] = jnp.broadcast_to(column(planck[...]), planck_out.shape)
    share_out[...] = jnp.broadcast_to(column(share[...]), share_out.shape)
    wide, fine = high.shape
    place = lax.broadcasted_iota(jnp.int32, (wide, fine), 0)
    total = jnp.zeros((wide, fine), f32)
    for k in range(stencil.shape[0]):
        at = stencil[k : k + 1, :]
        spot = jnp.where(at < RIM, wide - RIM + at, at - RIM)
        total = total + jnp.where(place == spot, weight[k : k + 1, :], 0.0)
    parts = split(total, 2)
    high[...] = parts[0]
    low[...] = parts[1]

    b = bias[...] * LOG2E
    lane = lax.broadcasted_iota(jnp.int32, b.shape, 1)
    for i in range(blocks):
        large[i].wait()
        for j in range(block):
            tail = jnp.where(lane == i * block + j, b, 0.0)
            parts = split(jnp.concatenate([absorb[i, :, j, :], tail], axis=1), 2)
            table[i * block + j, :, 0:depth] = parts[0]
            table[i * block + j, :, depth:double] = parts[1]


def prepare(absorb, bias, planck, share, stencil, weight, coarse):
    g, levels, feat = absorb.shape
    fine = stencil.shape[1]
    block = 8
    depth = feat + levels
    column = jax.ShapeDtypeStruct((g, coarse), f32)
    spread_table = jax.ShapeDtypeStruct((2 * coarse, fine), bf16)
    return pl.pallas_call(
        functools.partial(prepare_body, block),
        out_shape=(
            jax.ShapeDtypeStruct((levels, g, 2 * depth), bf16),
            column,
            column,
            spread_table,
            spread_table,
        ),
        in_specs=[HBM] * 6,
        out_specs=[VMEM] * 5,
        scratch_shapes=[
            pltpu.VMEM((levels // block, g, block, feat), f32),
            pltpu.VMEM(bias.shape, f32),
            pltpu.VMEM(planck.shape, f32),
            pltpu.VMEM(share.shape, f32),
            pltpu.VMEM(stencil.shape, jnp.int32),
            pltpu.VMEM(weight.shape, f32),
            pltpu.SemaphoreType.DMA((5 + levels // block,)),
        ],
        compiler_params=pltpu.CompilerParams(vmem_limit_bytes=28 * MIB),
        cost_estimate=pl.CostEstimate(
            flops=10 * g * levels * feat, bytes_accessed=8 * g * levels * depth, transcendentals=0
        ),
        name="prepare",
    )(*(stay(x) for x in (absorb, bias, planck, share, stencil, weight)))


def flux_body(block, scale, count, table, planck, share, *refs):
    chunks, outs, scratch = refs[:count], refs[count : 2 * count], refs[2 * count :]
    sweeps(block, scale, table, chunks, planck, share, outs, scratch)


def flux(table, planck, share, chunks, scale):
    levels, g, double = table.shape
    count, half = len(chunks), chunks[0].shape[1]
    block = 4
    return pl.pallas_call(
        functools.partial(flux_body, block, scale, count),
        out_shape=(jax.ShapeDtypeStruct((levels, half), f32),) * count,
        in_specs=[VMEM] * (3 + count),
        out_specs=(VMEM,) * count,
        scratch_shapes=sweep_scratch(block, g, levels, double // 2, count, half),
        compiler_params=pltpu.CompilerParams(vmem_limit_bytes=20 * MIB),
        cost_estimate=pl.CostEstimate(
            flops=3 * g * levels * double * count * half,
            bytes_accessed=2 * g * levels * double,
            transcendentals=3 * g * levels * count * half,
        ),
        name="flux",
    )(table, planck, share, *chunks)


def spread_body(own, first, second, parity, high, low, out):
    n = own.shape[1]
    lane = lax.broadcasted_iota(jnp.int32, own.shape, 1)
    late = jnp.where(lane >= n // 2, 1, 0)
    halo = jnp.where(late == parity[0], first[...], second[...])
    wide = jnp.concatenate([own[...], halo], axis=1)
    a, c = split(wide, 2)
    out[...] = dot(a, high[...]) + (dot(a, low[...]) + dot(c, high[...]))


def spread(own, first, second, parity, high, low):
    levels = own.shape[0]
    fine = high.shape[1]
    return pl.pallas_call(
        spread_body,
        out_shape=jax.ShapeDtypeStruct((levels, fine), f32),
        in_specs=[VMEM] * 3 + [pl.BlockSpec(memory_space=pltpu.SMEM)] + [VMEM] * 2,
        out_specs=VMEM,
        compiler_params=pltpu.CompilerParams(vmem_limit_bytes=16 * MIB),
        name="spread",
    )(own, first, second, parity, high, low)


def shards(
    state, cosine, grouping, sunlit, absorb, level_bias, planck, solar_share, stencil, stencil_weight
):
    fine, fields, levels = state.shape
    coarse = fine // 4
    n_sec = lax.axis_size("sec")
    devices = n_sec * lax.axis_size("col")
    columns = state.transpose(1, 2, 0).reshape(fields * levels, fine)
    rows = group(columns, cosine[None], grouping, sunlit)

    def swap(x, m):
        return lax.ppermute(x, "sec", [(i, i ^ m) for i in range(n_sec)])

    scale = 4.0 / (planck.shape[0] * n_sec)
    first, second = swap(rows, 1), swap(rows, 2)
    table, weight, share, near, far = prepare(
        absorb, level_bias, planck[None], solar_share[None], stencil, stencil_weight, coarse
    )
    later, table = lax.optimization_barrier((first, table))
    third = swap(later, 2)
    heats = flux(table, weight, share, [first, second], scale)
    third, table, *tied = lax.optimization_barrier((third, table, heats[0]))
    (heat,) = flux(table, weight, share, [third], scale)
    others = swap(tied[0], 1) + swap(heats[1], 2)
    others, heat, table, rows = lax.optimization_barrier((others, heat, table, rows))
    last = swap(heat, 3)
    (total,) = flux(table, weight, share, [rows], scale)
    total = total + others + last
    pairs = [(i, i ^ 1) for i in range(devices)]
    across = [(i, (i + 1) % devices if i % 2 else (i - 1) % devices) for i in range(devices)]
    second = lax.ppermute(total, ("sec", "col"), across)
    first = lax.ppermute(total, ("sec", "col"), pairs)
    parity = jnp.bitwise_and(lax.axis_index(("sec", "col")), 1).astype(jnp.int32).reshape(1)
    return spread(total, second, first, 1 - parity, near, far)


def solution(mesh):
    placed = (
        P(("sec", "col"), None, None),
        P(("sec", "col")),
        P(("sec", "col"), None),
        P(("sec", "col")),
        P("sec", None, None),
        P("sec", None),
        P("sec"),
        P("sec"),
        P(None, ("sec", "col")),
        P(None, ("sec", "col")),
    )
    return jax.shard_map(
        shards, mesh=mesh, in_specs=placed, out_specs=P(None, ("sec", "col")), check_vma=False
    )
```

```python
import functools

import jax
import jax.numpy as jnp
from jax import lax
from jax.experimental import pallas as pl
from jax.experimental.pallas import tpu as pltpu
from jax.sharding import PartitionSpec as P

RIM = 8
LOG2E = 1.4426950408889634
MIB = 1 << 20
bf16 = jnp.bfloat16
f32 = jnp.float32
VMEM = pl.BlockSpec(memory_space=pltpu.VMEM)


def split(x, parts):
    terms = []
    for _ in range(parts):
        term = x.astype(bf16)
        terms.append(term)
        x = x - term.astype(f32)
    return terms


def dot(a, b):
    return jnp.dot(a, b, preferred_element_type=f32)


HBM = pl.BlockSpec(memory_space=pltpu.HBM)


def stay(x):
    return pltpu.with_memory_space_constraint(x, pltpu.HBM)


def group_body(state_in, cosine_in, grouping_in, sunlit, out, state, cosine, grouping, sems):
    copies = [
        pltpu.make_async_copy(source, target, sems.at[i])
        for i, (source, target) in enumerate(
            ((grouping_in, grouping), (cosine_in, cosine), (state_in, state))
        )
    ]
    for copy in copies:
        copy.start()
    feat, fine = state.shape
    coarse = out.shape[1]
    place = lax.broadcasted_iota(jnp.int32, (fine, fine), 0)
    member = lax.broadcasted_iota(jnp.int32, (fine, coarse), 0) // 4
    home = lax.broadcasted_iota(jnp.int32, (fine, coarse), 1)
    mean = jnp.where(member == home, 0.25, 0.0).astype(bf16)
    copies[0].wait()
    picks = jnp.where(place == grouping[...], 1.0, 0.0).astype(bf16)
    weights = dot(picks, mean).astype(bf16)
    copies[1].wait()
    copies[2].wait()
    total = jnp.zeros((feat, coarse), f32)
    for term in split(state[...], 2)[::-1]:
        total = total + dot(term, weights)
    out[0:feat, :] = total
    light = jnp.zeros((8, coarse), f32)
    for term in split(jnp.broadcast_to(cosine[...], (8, fine)), 3)[::-1]:
        light = light + dot(term, weights)
    lane = lax.broadcasted_iota(jnp.int32, (8, coarse), 1)
    out[feat : feat + 8, :] = jnp.where(lane < sunlit[0], 4.0 * light, 0.0)


def group(state, cosine, grouping, sunlit):
    feat, fine = state.shape
    coarse = fine // 4
    return pl.pallas_call(
        group_body,
        out_shape=jax.ShapeDtypeStruct((feat + 8, coarse), f32),
        in_specs=[HBM, HBM, HBM, pl.BlockSpec(memory_space=pltpu.SMEM)],
        out_specs=VMEM,
        scratch_shapes=[
            pltpu.VMEM((feat, fine), f32),
            pltpu.VMEM((1, fine), f32),
            pltpu.VMEM((1, fine), jnp.int32),
            pltpu.SemaphoreType.DMA((3,)),
        ],
        compiler_params=pltpu.CompilerParams(vmem_limit_bytes=16 * MIB),
        cost_estimate=pl.CostEstimate(
            flops=8 * feat * fine * coarse, bytes_accessed=4 * feat * fine, transcendentals=0
        ),
        name="group",
    )(stay(state), stay(cosine), stay(grouping), sunlit)


def trans_of(y):
    low = lax.log2(1.0 + jnp.exp2(jnp.minimum(y, 64.0)))
    return jnp.exp2(-0.1 * jnp.maximum(low, y))


def sweeps(block, scale, span, table, chunks, planck, share, outs, scratch):
    right, zs, ts, downs, warms = scratch
    levels, _, double = table.shape
    low, high = span
    g = high - low
    depth = double // 2
    feat = depth - levels
    half = chunks[0].shape[1]
    count = len(chunks)
    n = count * half
    blocks = levels // block
    top = 0 if count == 1 else depth
    for i, rows in enumerate(chunks):
        lanes = slice(half * i, half * (i + 1))
        under = slice(half, 2 * half) if count == 1 else lanes
        parts = split(rows[0:feat, :] * LOG2E, 2)
        right[0:feat, lanes] = parts[0]
        right[top : top + feat, under] = parts[1]
        warms[0:levels, lanes] = 2.0 + jnp.tanh(rows[0:levels, :])
        right[feat:depth, lanes] = jnp.ones((levels, half), bf16)
        right[top + feat : top + depth, under] = jnp.zeros((levels, half), bf16)
    warms[levels : levels + 8, :] = jnp.zeros((8, n), f32)

    def fold(x):
        return jnp.sum(x.reshape(g // 8, 8, n), axis=0)

    def absorb(b):
        a = table[b * block : (b + 1) * block, low:high].reshape(block * g, double)
        c = right[0:depth, :]
        z = dot(a[:, 0:depth], c) + dot(a[:, depth:double], c)
        if count == 1:
            zs[b % 2] = z[:, 0:n] + z[:, n : 2 * n]
        else:
            zs[b % 2] = z + dot(a[:, 0:depth], right[depth:double, :])

    absorb(0)
    weight = jnp.concatenate([planck[low:high, :]] * count, axis=1)
    lights = jnp.concatenate([rows[feat : feat + 1, :] for rows in chunks], axis=1)
    d = jnp.concatenate([share[low:high, :]] * count, axis=1) * lights - weight * warms[0:1, :]
    downs[0] = fold(d)
    for b in range(blocks):
        if b + 1 < blocks:
            absorb(b + 1)
        for j in range(block):
            l = b * block + j
            t = trans_of(zs[b % 2, j * g : (j + 1) * g, :])
            ts[l] = t
            d = t * d + weight * (warms[l : l + 1, :] - warms[l + 1 : l + 2, :])
            downs[l + 1] = fold(d)
    v = 0.3 * d

    def climb(i, carry):
        v, below = carry
        l = levels - 1 - i
        rise = warms[pl.ds(l, 1), :] - warms[pl.ds(jnp.maximum(l - 1, 0), 1), :]
        v = ts[l] * v + weight * rise
        above = fold(v)
        downs[l + 1] = (downs[l] - downs[l + 1]) + (below - above)
        return v, above

    lax.fori_loop(0, levels, climb, (v, fold(v)), unroll=8)
    heat = downs[1 : levels + 1, 0, :]
    for s in range(1, 8):
        heat = heat + downs[1 : levels + 1, s, :]
    here = warms[0:levels, :]
    prior = jnp.concatenate([here[0:1], here[0 : levels - 1]], axis=0)
    total = jnp.sum(fold(weight), axis=0, keepdims=True)
    heat = scale * (heat + total * ((here - warms[1 : levels + 1, :]) + (here - prior)))
    for i, out in enumerate(outs):
        out[...] = heat[:, half * i : half * (i + 1)]


def sweep_scratch(block, g, levels, depth, count, half):
    n = count * half
    return [
        pltpu.VMEM((depth, 2 * n) if count == 1 else (2 * depth, n), bf16),
        pltpu.VMEM((2, block * g, n), f32),
        pltpu.VMEM((levels, g, n), f32),
        pltpu.VMEM((levels + 1, 8, n), f32),
        pltpu.VMEM((levels + 8, n), f32),
    ]


def prepare_body(
    block,
    absorb_in,
    bias_in,
    planck_in,
    share_in,
    stencil_in,
    weight_in,
    table,
    planck_out,
    share_out,
    high,
    low,
    absorb,
    bias,
    planck,
    share,
    stencil,
    weight,
    sems,
):
    levels, g, double = table.shape
    depth = double // 2
    blocks = levels // block
    small = [
        pltpu.make_async_copy(source, target, sems.at[i])
        for i, (source, target) in enumerate(
            (
                (bias_in, bias),
                (planck_in, planck),
                (share_in, share),
                (stencil_in, stencil),
                (weight_in, weight),
            )
        )
    ]
    large = [
        pltpu.make_async_copy(
            absorb_in.at[:, pl.ds(i * block, block), :], absorb.at[i], sems.at[len(small) + i]
        )
        for i in range(blocks)
    ]
    for copy in small + large:
        copy.start()
    for copy in small:
        copy.wait()

    def column(row):
        n = row.shape[1]
        eye = lax.broadcasted_iota(jnp.int32, (n, n), 0) == lax.broadcasted_iota(
            jnp.int32, (n, n), 1
        )
        return jnp.sum(jnp.where(eye, row, 0.0), axis=1, keepdims=True)

    planck_out[...] = jnp.broadcast_to(column(planck[...]), planck_out.shape)
    share_out[...] = jnp.broadcast_to(column(share[...]), share_out.shape)
    wide, fine = high.shape
    place = lax.broadcasted_iota(jnp.int32, (wide, fine), 0)
    total = jnp.zeros((wide, fine), f32)
    for k in range(stencil.shape[0]):
        at = stencil[k : k + 1, :]
        spot = jnp.where(at < RIM, wide - RIM + at, at - RIM)
        total = total + jnp.where(place == spot, weight[k : k + 1, :], 0.0)
    parts = split(total, 2)
    high[...] = parts[0]
    low[...] = parts[1]

    b = bias[...] * LOG2E
    lane = lax.broadcasted_iota(jnp.int32, b.shape, 1)
    for i in range(blocks):
        large[i].wait()
        for j in range(block):
            tail = jnp.where(lane == i * block + j, b, 0.0)
            parts = split(jnp.concatenate([absorb[i, :, j, :], tail], axis=1), 2)
            table[i * block + j, :, 0:depth] = parts[0]
            table[i * block + j, :, depth:double] = parts[1]


def prepare(absorb, bias, planck, share, stencil, weight, coarse):
    g, levels, feat = absorb.shape
    fine = stencil.shape[1]
    block = 8
    depth = feat + levels
    column = jax.ShapeDtypeStruct((g, coarse), f32)
    spread_table = jax.ShapeDtypeStruct((2 * coarse, fine), bf16)
    return pl.pallas_call(
        functools.partial(prepare_body, block),
        out_shape=(
            jax.ShapeDtypeStruct((levels, g, 2 * depth), bf16),
            column,
            column,
            spread_table,
            spread_table,
        ),
        in_specs=[HBM] * 6,
        out_specs=[VMEM] * 5,
        scratch_shapes=[
            pltpu.VMEM((levels // block, g, block, feat), f32),
            pltpu.VMEM(bias.shape, f32),
            pltpu.VMEM(planck.shape, f32),
            pltpu.VMEM(share.shape, f32),
            pltpu.VMEM(stencil.shape, jnp.int32),
            pltpu.VMEM(weight.shape, f32),
            pltpu.SemaphoreType.DMA((5 + levels // block,)),
        ],
        compiler_params=pltpu.CompilerParams(vmem_limit_bytes=28 * MIB),
        cost_estimate=pl.CostEstimate(
            flops=10 * g * levels * feat, bytes_accessed=8 * g * levels * depth, transcendentals=0
        ),
        name="prepare",
    )(*(stay(x) for x in (absorb, bias, planck, share, stencil, weight)))


def flux_body(block, scale, span, count, table, planck, share, *refs):
    chunks, outs, scratch = refs[:count], refs[count : 2 * count], refs[2 * count :]
    sweeps(block, scale, span, table, chunks, planck, share, outs, scratch)


def flux(table, planck, share, chunks, scale, span=None):
    levels, g, double = table.shape
    span = span or (0, g)
    g = span[1] - span[0]
    count, half = len(chunks), chunks[0].shape[1]
    block = 4 if count == 2 or 2 * g > table.shape[1] else 8
    return pl.pallas_call(
        functools.partial(flux_body, block, scale, span, count),
        out_shape=(jax.ShapeDtypeStruct((levels, half), f32),) * count,
        in_specs=[VMEM] * (3 + count),
        out_specs=(VMEM,) * count,
        scratch_shapes=sweep_scratch(block, g, levels, double // 2, count, half),
        compiler_params=pltpu.CompilerParams(vmem_limit_bytes=20 * MIB),
        cost_estimate=pl.CostEstimate(
            flops=3 * g * levels * double * count * half,
            bytes_accessed=2 * g * levels * double,
            transcendentals=3 * g * levels * count * half,
        ),
        name="flux",
    )(table, planck, share, *chunks)


def spread_body(own, first, second, parity, high, low, out):
    n = own.shape[1]
    lane = lax.broadcasted_iota(jnp.int32, own.shape, 1)
    late = jnp.where(lane >= n // 2, 1, 0)
    halo = jnp.where(late == parity[0], first[...], second[...])
    wide = jnp.concatenate([own[...], halo], axis=1)
    a, c = split(wide, 2)
    both = dot(jnp.concatenate([a, c], axis=0), high[...])
    m = a.shape[0]
    out[...] = both[0:m] + (dot(a, low[...]) + both[m : 2 * m])


def spread(own, first, second, parity, high, low):
    levels = own.shape[0]
    fine = high.shape[1]
    return pl.pallas_call(
        spread_body,
        out_shape=jax.ShapeDtypeStruct((levels, fine), f32),
        in_specs=[VMEM] * 3 + [pl.BlockSpec(memory_space=pltpu.SMEM)] + [VMEM] * 2,
        out_specs=VMEM,
        compiler_params=pltpu.CompilerParams(vmem_limit_bytes=16 * MIB),
        name="spread",
    )(own, first, second, parity, high, low)


def shards(
    state, cosine, grouping, sunlit, absorb, level_bias, planck, solar_share, stencil, stencil_weight
):
    fine, fields, levels = state.shape
    coarse = fine // 4
    n_sec = lax.axis_size("sec")
    devices = n_sec * lax.axis_size("col")
    columns = state.transpose(1, 2, 0).reshape(fields * levels, fine)
    rows = group(columns, cosine[None], grouping, sunlit)

    def swap(x, m):
        return lax.ppermute(x, "sec", [(i, i ^ m) for i in range(n_sec)])

    scale = 4.0 / (planck.shape[0] * n_sec)
    first, second = swap(rows, 1), swap(rows, 2)
    table, weight, share, near, far = prepare(
        absorb, level_bias, planck[None], solar_share[None], stencil, stencil_weight, coarse
    )
    later, table = lax.optimization_barrier((first, table))
    third = swap(later, 2)
    heats = flux(table, weight, share, [first, second], scale)
    third, table, *heats = lax.optimization_barrier((third, table, *heats))
    (heat,) = flux(table, weight, share, [third], scale)
    heat, table, rows, *heats = lax.optimization_barrier((heat, table, rows, *heats))
    (total,) = flux(table, weight, share, [rows], scale)
    total = swap(heat, 3) + swap(heats[0], 1) + swap(heats[1], 2) + total
    pairs = [(i, i ^ 1) for i in range(devices)]
    across = [(i, (i + 1) % devices if i % 2 else (i - 1) % devices) for i in range(devices)]
    second = lax.ppermute(total, ("sec", "col"), across)
    first = lax.ppermute(total, ("sec", "col"), pairs)
    parity = jnp.bitwise_and(lax.axis_index(("sec", "col")), 1).astype(jnp.int32).reshape(1)
    return spread(total, second, first, 1 - parity, near, far)


def solution(mesh):
    placed = (
        P(("sec", "col"), None, None),
        P(("sec", "col")),
        P(("sec", "col"), None),
        P(("sec", "col")),
        P("sec", None, None),
        P("sec", None),
        P("sec"),
        P("sec"),
        P(None, ("sec", "col")),
        P(None, ("sec", "col")),
    )
    return jax.shard_map(
        shards, mesh=mesh, in_specs=placed, out_specs=P(None, ("sec", "col")), check_vma=False
    )
```

```python
import functools

import jax
import jax.numpy as jnp
from jax import lax
from jax.experimental import pallas as pl
from jax.experimental.pallas import tpu as pltpu
from jax.sharding import PartitionSpec as P

RIM = 8
LOG2E = 1.4426950408889634
MIB = 1 << 20
bf16 = jnp.bfloat16
f32 = jnp.float32
VMEM = pl.BlockSpec(memory_space=pltpu.VMEM)


def split(x, parts):
    terms = []
    for _ in range(parts):
        term = x.astype(bf16)
        terms.append(term)
        x = x - term.astype(f32)
    return terms


def dot(a, b):
    return jnp.dot(a, b, preferred_element_type=f32)


HBM = pl.BlockSpec(memory_space=pltpu.HBM)


def stay(x):
    return pltpu.with_memory_space_constraint(x, pltpu.HBM)


def group_body(state_in, cosine_in, grouping_in, sunlit, out, state, cosine, grouping, sems):
    copies = [
        pltpu.make_async_copy(source, target, sems.at[i])
        for i, (source, target) in enumerate(
            ((grouping_in, grouping), (cosine_in, cosine), (state_in, state))
        )
    ]
    for copy in copies:
        copy.start()
    feat, fine = state.shape
    coarse = out.shape[1]
    place = lax.broadcasted_iota(jnp.int32, (fine, fine), 0)
    member = lax.broadcasted_iota(jnp.int32, (fine, coarse), 0) // 4
    home = lax.broadcasted_iota(jnp.int32, (fine, coarse), 1)
    mean = jnp.where(member == home, 0.25, 0.0).astype(bf16)
    copies[0].wait()
    picks = jnp.where(place == grouping[...], 1.0, 0.0).astype(bf16)
    weights = dot(picks, mean).astype(bf16)
    copies[1].wait()
    copies[2].wait()
    total = jnp.zeros((feat, coarse), f32)
    for term in split(state[...], 2)[::-1]:
        total = total + dot(term, weights)
    out[0:feat, :] = total
    light = jnp.zeros((8, coarse), f32)
    for term in split(jnp.broadcast_to(cosine[...], (8, fine)), 3)[::-1]:
        light = light + dot(term, weights)
    lane = lax.broadcasted_iota(jnp.int32, (8, coarse), 1)
    out[feat : feat + 8, :] = jnp.where(lane < sunlit[0], 4.0 * light, 0.0)


def group(state, cosine, grouping, sunlit):
    feat, fine = state.shape
    coarse = fine // 4
    return pl.pallas_call(
        group_body,
        out_shape=jax.ShapeDtypeStruct((feat + 8, coarse), f32),
        in_specs=[HBM, HBM, HBM, pl.BlockSpec(memory_space=pltpu.SMEM)],
        out_specs=VMEM,
        scratch_shapes=[
            pltpu.VMEM((feat, fine), f32),
            pltpu.VMEM((1, fine), f32),
            pltpu.VMEM((1, fine), jnp.int32),
            pltpu.SemaphoreType.DMA((3,)),
        ],
        compiler_params=pltpu.CompilerParams(vmem_limit_bytes=16 * MIB),
        cost_estimate=pl.CostEstimate(
            flops=8 * feat * fine * coarse, bytes_accessed=4 * feat * fine, transcendentals=0
        ),
        name="group",
    )(stay(state), stay(cosine), stay(grouping), sunlit)


def trans_of(y):
    low = lax.log2(1.0 + jnp.exp2(jnp.minimum(y, 64.0)))
    return jnp.exp2(-0.1 * jnp.maximum(low, y))


def sweeps(block, scale, span, table, chunks, planck, share, outs, scratch):
    right, zs, ts, downs, warms = scratch
    levels, _, double = table.shape
    low, high = span
    g = high - low
    depth = double // 2
    feat = depth - levels
    half = chunks[0].shape[1]
    count = len(chunks)
    n = count * half
    blocks = levels // block
    top = 0 if count == 1 else depth
    for i, rows in enumerate(chunks):
        lanes = slice(half * i, half * (i + 1))
        under = slice(half, 2 * half) if count == 1 else lanes
        parts = split(rows[0:feat, :] * LOG2E, 2)
        right[0:feat, lanes] = parts[0]
        right[top : top + feat, under] = parts[1]
        warms[0:levels, lanes] = 2.0 + jnp.tanh(rows[0:levels, :])
        right[feat:depth, lanes] = jnp.ones((levels, half), bf16)
        right[top + feat : top + depth, under] = jnp.zeros((levels, half), bf16)
    warms[levels : levels + 8, :] = jnp.zeros((8, n), f32)

    def fold(x):
        return jnp.sum(x.reshape(g // 8, 8, n), axis=0)

    def absorb(b):
        a = table[b * block : (b + 1) * block, low:high].reshape(block * g, double)
        c = right[0:depth, :]
        z = dot(a[:, 0:depth], c) + dot(a[:, depth:double], c)
        if count == 1:
            zs[b % 2] = z[:, 0:n] + z[:, n : 2 * n]
        else:
            zs[b % 2] = z + dot(a[:, 0:depth], right[depth:double, :])

    absorb(0)
    weight = jnp.concatenate([planck[low:high, :]] * count, axis=1)
    lights = jnp.concatenate([rows[feat : feat + 1, :] for rows in chunks], axis=1)
    d = jnp.concatenate([share[low:high, :]] * count, axis=1) * lights - weight * warms[0:1, :]
    downs[0] = fold(d)
    for b in range(blocks):
        if b + 1 < blocks:
            absorb(b + 1)
        for j in range(block):
            l = b * block + j
            t = trans_of(zs[b % 2, j * g : (j + 1) * g, :])
            ts[l] = t
            d = t * d + weight * (warms[l : l + 1, :] - warms[l + 1 : l + 2, :])
            downs[l + 1] = fold(d)
    v = 0.3 * d

    def climb(i, carry):
        v, below = carry
        l = levels - 1 - i
        rise = warms[pl.ds(l, 1), :] - warms[pl.ds(jnp.maximum(l - 1, 0), 1), :]
        v = ts[l] * v + weight * rise
        above = fold(v)
        downs[l + 1] = (downs[l] - downs[l + 1]) + (below - above)
        return v, above

    lax.fori_loop(0, levels, climb, (v, fold(v)), unroll=16)
    heat = downs[1 : levels + 1, 0, :]
    for s in range(1, 8):
        heat = heat + downs[1 : levels + 1, s, :]
    here = warms[0:levels, :]
    prior = jnp.concatenate([here[0:1], here[0 : levels - 1]], axis=0)
    total = jnp.sum(fold(weight), axis=0, keepdims=True)
    heat = scale * (heat + total * ((here - warms[1 : levels + 1, :]) + (here - prior)))
    for i, out in enumerate(outs):
        out[...] = heat[:, half * i : half * (i + 1)]


def sweep_scratch(block, g, levels, depth, count, half):
    n = count * half
    return [
        pltpu.VMEM((depth, 2 * n) if count == 1 else (2 * depth, n), bf16),
        pltpu.VMEM((2, block * g, n), f32),
        pltpu.VMEM((levels, g, n), f32),
        pltpu.VMEM((levels + 1, 8, n), f32),
        pltpu.VMEM((levels + 8, n), f32),
    ]


def prepare_body(
    block,
    absorb_in,
    bias_in,
    planck_in,
    share_in,
    stencil_in,
    weight_in,
    table,
    planck_out,
    share_out,
    high,
    low,
    absorb,
    bias,
    planck,
    share,
    stencil,
    weight,
    sems,
):
    levels, g, double = table.shape
    depth = double // 2
    blocks = levels // block
    small = [
        pltpu.make_async_copy(source, target, sems.at[i])
        for i, (source, target) in enumerate(
            (
                (bias_in, bias),
                (planck_in, planck),
                (share_in, share),
                (stencil_in, stencil),
                (weight_in, weight),
            )
        )
    ]
    large = [
        pltpu.make_async_copy(
            absorb_in.at[:, pl.ds(i * block, block), :], absorb.at[i], sems.at[len(small) + i]
        )
        for i in range(blocks)
    ]
    for copy in small + large:
        copy.start()
    for copy in small:
        copy.wait()

    def column(row):
        n = row.shape[1]
        eye = lax.broadcasted_iota(jnp.int32, (n, n), 0) == lax.broadcasted_iota(
            jnp.int32, (n, n), 1
        )
        return jnp.sum(jnp.where(eye, row, 0.0), axis=1, keepdims=True)

    planck_out[...] = jnp.broadcast_to(column(planck[...]), planck_out.shape)
    share_out[...] = jnp.broadcast_to(column(share[...]), share_out.shape)
    wide, fine = high.shape
    place = lax.broadcasted_iota(jnp.int32, (wide, fine), 0)
    total = jnp.zeros((wide, fine), f32)
    for k in range(stencil.shape[0]):
        at = stencil[k : k + 1, :]
        spot = jnp.where(at < RIM, wide - RIM + at, at - RIM)
        total = total + jnp.where(place == spot, weight[k : k + 1, :], 0.0)
    parts = split(total, 2)
    high[...] = parts[0]
    low[...] = parts[1]

    b = bias[...] * LOG2E
    lane = lax.broadcasted_iota(jnp.int32, b.shape, 1)
    for i in range(blocks):
        large[i].wait()
        for j in range(block):
            tail = jnp.where(lane == i * block + j, b, 0.0)
            parts = split(jnp.concatenate([absorb[i, :, j, :], tail], axis=1), 2)
            table[i * block + j, :, 0:depth] = parts[0]
            table[i * block + j, :, depth:double] = parts[1]


def prepare(absorb, bias, planck, share, stencil, weight, coarse):
    g, levels, feat = absorb.shape
    fine = stencil.shape[1]
    block = 8
    depth = feat + levels
    column = jax.ShapeDtypeStruct((g, coarse), f32)
    spread_table = jax.ShapeDtypeStruct((2 * coarse, fine), bf16)
    return pl.pallas_call(
        functools.partial(prepare_body, block),
        out_shape=(
            jax.ShapeDtypeStruct((levels, g, 2 * depth), bf16),
            column,
            column,
            spread_table,
            spread_table,
        ),
        in_specs=[HBM] * 6,
        out_specs=[VMEM] * 5,
        scratch_shapes=[
            pltpu.VMEM((levels // block, g, block, feat), f32),
            pltpu.VMEM(bias.shape, f32),
            pltpu.VMEM(planck.shape, f32),
            pltpu.VMEM(share.shape, f32),
            pltpu.VMEM(stencil.shape, jnp.int32),
            pltpu.VMEM(weight.shape, f32),
            pltpu.SemaphoreType.DMA((5 + levels // block,)),
        ],
        compiler_params=pltpu.CompilerParams(vmem_limit_bytes=28 * MIB),
        cost_estimate=pl.CostEstimate(
            flops=10 * g * levels * feat, bytes_accessed=8 * g * levels * depth, transcendentals=0
        ),
        name="prepare",
    )(*(stay(x) for x in (absorb, bias, planck, share, stencil, weight)))


def flux_body(block, scale, span, count, table, planck, share, *refs):
    chunks, outs, scratch = refs[:count], refs[count : 2 * count], refs[2 * count :]
    sweeps(block, scale, span, table, chunks, planck, share, outs, scratch)


def flux(table, planck, share, chunks, scale, span=None):
    levels, g, double = table.shape
    span = span or (0, g)
    g = span[1] - span[0]
    count, half = len(chunks), chunks[0].shape[1]
    block = 4 if count == 2 or 2 * g > table.shape[1] else 8
    return pl.pallas_call(
        functools.partial(flux_body, block, scale, span, count),
        out_shape=(jax.ShapeDtypeStruct((levels, half), f32),) * count,
        in_specs=[VMEM] * (3 + count),
        out_specs=(VMEM,) * count,
        scratch_shapes=sweep_scratch(block, g, levels, double // 2, count, half),
        compiler_params=pltpu.CompilerParams(vmem_limit_bytes=20 * MIB),
        cost_estimate=pl.CostEstimate(
            flops=3 * g * levels * double * count * half,
            bytes_accessed=2 * g * levels * double,
            transcendentals=3 * g * levels * count * half,
        ),
        name="flux",
    )(table, planck, share, *chunks)


def products(x, high, low):
    a, c = split(x, 2)
    m = x.shape[0]
    both = dot(jnp.concatenate([a, c], axis=0), high)
    return both[0:m] + (dot(a, low) + both[m : 2 * m])


def inner_body(own, high, low, out):
    n = own.shape[1]
    out[...] = products(own[...], high[0:n, :], low[0:n, :])


def edge_body(inner, first, second, parity, high, low, out):
    n = first.shape[1]
    fine = out.shape[1]
    lane = lax.broadcasted_iota(jnp.int32, first.shape, 1)
    late = jnp.where(lane >= n // 2, 1, 0)
    halo = jnp.where(late == parity[0], first[...], second[...])
    parts = [
        jnp.concatenate([t[n : 2 * n, 0:128], t[n : 2 * n, fine - 128 : fine]], axis=1)
        for t in (high, low)
    ]
    added = products(halo, *parts)
    out[:, 0:128] = inner[:, 0:128] + added[:, 0:128]
    out[:, 128 : fine - 128] = inner[:, 128 : fine - 128]
    out[:, fine - 128 : fine] = inner[:, fine - 128 : fine] + added[:, 128:256]


def spread_inner(own, high, low):
    levels = own.shape[0]
    fine = high.shape[1]
    return pl.pallas_call(
        inner_body,
        out_shape=jax.ShapeDtypeStruct((levels, fine), f32),
        in_specs=[VMEM] * 3,
        out_specs=VMEM,
        compiler_params=pltpu.CompilerParams(vmem_limit_bytes=16 * MIB),
        cost_estimate=pl.CostEstimate(
            flops=6 * levels * own.shape[1] * fine, bytes_accessed=4 * levels * fine, transcendentals=0
        ),
        name="spread_inner",
    )(own, high, low)


def spread(inner, first, second, parity, high, low):
    return pl.pallas_call(
        edge_body,
        out_shape=jax.ShapeDtypeStruct(inner.shape, f32),
        in_specs=[VMEM] * 3 + [pl.BlockSpec(memory_space=pltpu.SMEM)] + [VMEM] * 2,
        out_specs=VMEM,
        compiler_params=pltpu.CompilerParams(vmem_limit_bytes=16 * MIB),
        name="spread",
    )(inner, first, second, parity, high, low)


def shards(
    state, cosine, grouping, sunlit, absorb, level_bias, planck, solar_share, stencil, stencil_weight
):
    fine, fields, levels = state.shape
    coarse = fine // 4
    n_sec = lax.axis_size("sec")
    devices = n_sec * lax.axis_size("col")
    columns = state.transpose(1, 2, 0).reshape(fields * levels, fine)
    rows = group(columns, cosine[None], grouping, sunlit)

    def swap(x, m):
        return lax.ppermute(x, "sec", [(i, i ^ m) for i in range(n_sec)])

    scale = 4.0 / (planck.shape[0] * n_sec)
    first, second = swap(rows, 1), swap(rows, 2)
    table, weight, share, near, far = prepare(
        absorb, level_bias, planck[None], solar_share[None], stencil, stencil_weight, coarse
    )
    later, table = lax.optimization_barrier((first, table))
    third = swap(later, 2)
    heats = flux(table, weight, share, [first, second], scale)
    third, table, *heats = lax.optimization_barrier((third, table, *heats))
    (heat,) = flux(table, weight, share, [third], scale)
    heat, table, rows, *heats = lax.optimization_barrier((heat, table, rows, *heats))
    (total,) = flux(table, weight, share, [rows], scale)
    total = swap(heats[0], 1) + swap(heat, 3) + swap(heats[1], 2) + total
    pairs = [(i, i ^ 1) for i in range(devices)]
    across = [(i, (i + 1) % devices if i % 2 else (i - 1) % devices) for i in range(devices)]
    second = lax.ppermute(total, ("sec", "col"), across)
    first = lax.ppermute(total, ("sec", "col"), pairs)
    parity = jnp.bitwise_and(lax.axis_index(("sec", "col")), 1).astype(jnp.int32).reshape(1)
    return spread(spread_inner(total, near, far), second, first, 1 - parity, near, far)


def solution(mesh):
    placed = (
        P(("sec", "col"), None, None),
        P(("sec", "col")),
        P(("sec", "col"), None),
        P(("sec", "col")),
        P("sec", None, None),
        P("sec", None),
        P("sec"),
        P("sec"),
        P(None, ("sec", "col")),
        P(None, ("sec", "col")),
    )
    return jax.shard_map(
        shards, mesh=mesh, in_specs=placed, out_specs=P(None, ("sec", "col")), check_vma=False
    )
```

```python
import functools

import jax
import jax.numpy as jnp
from jax import lax
from jax.experimental import pallas as pl
from jax.experimental.pallas import tpu as pltpu
from jax.sharding import PartitionSpec as P

RIM = 8
LOG2E = 1.4426950408889634
MIB = 1 << 20
bf16 = jnp.bfloat16
f32 = jnp.float32
VMEM = pl.BlockSpec(memory_space=pltpu.VMEM)


def split(x, parts):
    terms = []
    for _ in range(parts):
        term = x.astype(bf16)
        terms.append(term)
        x = x - term.astype(f32)
    return terms


def dot(a, b):
    return jnp.dot(a, b, preferred_element_type=f32)


HBM = pl.BlockSpec(memory_space=pltpu.HBM)


def stay(x):
    return pltpu.with_memory_space_constraint(x, pltpu.HBM)


def group_body(state_in, cosine_in, grouping_in, sunlit, out, state, cosine, grouping, sems):
    copies = [
        pltpu.make_async_copy(source, target, sems.at[i])
        for i, (source, target) in enumerate(
            ((grouping_in, grouping), (cosine_in, cosine), (state_in, state))
        )
    ]
    for copy in copies:
        copy.start()
    feat, fine = state.shape
    coarse = out.shape[1]
    place = lax.broadcasted_iota(jnp.int32, (fine, fine), 0)
    member = lax.broadcasted_iota(jnp.int32, (fine, coarse), 0) // 4
    home = lax.broadcasted_iota(jnp.int32, (fine, coarse), 1)
    mean = jnp.where(member == home, 0.25, 0.0).astype(bf16)
    copies[0].wait()
    picks = jnp.where(place == grouping[...], 1.0, 0.0).astype(bf16)
    weights = dot(picks, mean).astype(bf16)
    copies[1].wait()
    copies[2].wait()
    total = jnp.zeros((feat, coarse), f32)
    for term in split(state[...], 2)[::-1]:
        total = total + dot(term, weights)
    out[0:feat, :] = total
    light = jnp.zeros((8, coarse), f32)
    for term in split(jnp.broadcast_to(cosine[...], (8, fine)), 3)[::-1]:
        light = light + dot(term, weights)
    lane = lax.broadcasted_iota(jnp.int32, (8, coarse), 1)
    out[feat : feat + 8, :] = jnp.where(lane < sunlit[0], 4.0 * light, 0.0)


def group(state, cosine, grouping, sunlit):
    feat, fine = state.shape
    coarse = fine // 4
    return pl.pallas_call(
        group_body,
        out_shape=jax.ShapeDtypeStruct((feat + 8, coarse), f32),
        in_specs=[HBM, HBM, HBM, pl.BlockSpec(memory_space=pltpu.SMEM)],
        out_specs=VMEM,
        scratch_shapes=[
            pltpu.VMEM((feat, fine), f32),
            pltpu.VMEM((1, fine), f32),
            pltpu.VMEM((1, fine), jnp.int32),
            pltpu.SemaphoreType.DMA((3,)),
        ],
        compiler_params=pltpu.CompilerParams(vmem_limit_bytes=16 * MIB),
        cost_estimate=pl.CostEstimate(
            flops=8 * feat * fine * coarse, bytes_accessed=4 * feat * fine, transcendentals=0
        ),
        name="group",
    )(stay(state), stay(cosine), stay(grouping), sunlit)


def trans_of(y):
    low = lax.log2(1.0 + jnp.exp2(jnp.minimum(y, 64.0)))
    return jnp.exp2(-0.1 * jnp.maximum(low, y))


def sweeps(block, scale, span, table, chunks, planck, share, outs, scratch):
    right, zs, ts, downs, warms = scratch
    levels, _, double = table.shape
    low, high = span
    g = high - low
    depth = double // 2
    feat = depth - levels
    half = chunks[0].shape[1]
    count = len(chunks)
    n = count * half
    blocks = levels // block
    top = 0 if count == 1 else depth
    for i, rows in enumerate(chunks):
        lanes = slice(half * i, half * (i + 1))
        under = slice(half, 2 * half) if count == 1 else lanes
        parts = split(rows[0:feat, :] * LOG2E, 2)
        right[0:feat, lanes] = parts[0]
        right[top : top + feat, under] = parts[1]
        warms[0:levels, lanes] = 2.0 + jnp.tanh(rows[0:levels, :])
        right[feat:depth, lanes] = jnp.ones((levels, half), bf16)
        right[top + feat : top + depth, under] = jnp.zeros((levels, half), bf16)
    warms[levels : levels + 8, :] = jnp.zeros((8, n), f32)

    def fold(x):
        return jnp.sum(x.reshape(g // 8, 8, n), axis=0)

    def absorb(b):
        a = table[b * block : (b + 1) * block, low:high].reshape(block * g, double)
        c = right[0:depth, :]
        z = dot(a[:, 0:depth], c) + dot(a[:, depth:double], c)
        if count == 1:
            zs[b % 2] = z[:, 0:n] + z[:, n : 2 * n]
        else:
            zs[b % 2] = z + dot(a[:, 0:depth], right[depth:double, :])

    absorb(0)
    weight = jnp.concatenate([planck[low:high, :]] * count, axis=1)
    lights = jnp.concatenate([rows[feat : feat + 1, :] for rows in chunks], axis=1)
    d = jnp.concatenate([share[low:high, :]] * count, axis=1) * lights - weight * warms[0:1, :]
    downs[0] = fold(d)
    for b in range(blocks):
        if b + 1 < blocks:
            absorb(b + 1)
        for j in range(block):
            l = b * block + j
            t = trans_of(zs[b % 2, j * g : (j + 1) * g, :])
            ts[l] = t
            d = t * d + weight * (warms[l : l + 1, :] - warms[l + 1 : l + 2, :])
            downs[l + 1] = fold(d)
    v = 0.3 * d

    def climb(i, carry):
        v, below = carry
        l = levels - 1 - i
        rise = warms[pl.ds(l, 1), :] - warms[pl.ds(jnp.maximum(l - 1, 0), 1), :]
        v = ts[l] * v + weight * rise
        above = fold(v)
        downs[l + 1] = (downs[l] - downs[l + 1]) + (below - above)
        return v, above

    lax.fori_loop(0, levels, climb, (v, fold(v)), unroll=16)
    heat = downs[1 : levels + 1, 0, :]
    for s in range(1, 8):
        heat = heat + downs[1 : levels + 1, s, :]
    here = warms[0:levels, :]
    prior = jnp.concatenate([here[0:1], here[0 : levels - 1]], axis=0)
    total = jnp.sum(fold(weight), axis=0, keepdims=True)
    heat = scale * (heat + total * ((here - warms[1 : levels + 1, :]) + (here - prior)))
    for i, out in enumerate(outs):
        out[...] = heat[:, half * i : half * (i + 1)]


def sweep_scratch(block, g, levels, depth, count, half):
    n = count * half
    return [
        pltpu.VMEM((depth, 2 * n) if count == 1 else (2 * depth, n), bf16),
        pltpu.VMEM((2, block * g, n), f32),
        pltpu.VMEM((levels, g, n), f32),
        pltpu.VMEM((levels + 1, 8, n), f32),
        pltpu.VMEM((levels + 8, n), f32),
    ]


def prepare_body(
    block,
    absorb_in,
    bias_in,
    planck_in,
    share_in,
    stencil_in,
    weight_in,
    table,
    planck_out,
    share_out,
    high,
    low,
    absorb,
    bias,
    planck,
    share,
    stencil,
    weight,
    sems,
):
    levels, g, double = table.shape
    depth = double // 2
    blocks = levels // block
    small = [
        pltpu.make_async_copy(source, target, sems.at[i])
        for i, (source, target) in enumerate(
            (
                (bias_in, bias),
                (planck_in, planck),
                (share_in, share),
                (stencil_in, stencil),
                (weight_in, weight),
            )
        )
    ]
    large = [
        pltpu.make_async_copy(
            absorb_in.at[:, pl.ds(i * block, block), :], absorb.at[i], sems.at[len(small) + i]
        )
        for i in range(blocks)
    ]
    for copy in small + large:
        copy.start()
    for copy in small:
        copy.wait()

    def column(row):
        n = row.shape[1]
        eye = lax.broadcasted_iota(jnp.int32, (n, n), 0) == lax.broadcasted_iota(
            jnp.int32, (n, n), 1
        )
        return jnp.sum(jnp.where(eye, row, 0.0), axis=1, keepdims=True)

    planck_out[...] = jnp.broadcast_to(column(planck[...]), planck_out.shape)
    share_out[...] = jnp.broadcast_to(column(share[...]), share_out.shape)
    wide, fine = high.shape
    place = lax.broadcasted_iota(jnp.int32, (wide, fine), 0)
    total = jnp.zeros((wide, fine), f32)
    for k in range(stencil.shape[0]):
        at = stencil[k : k + 1, :]
        spot = jnp.where(at < RIM, wide - RIM + at, at - RIM)
        total = total + jnp.where(place == spot, weight[k : k + 1, :], 0.0)
    parts = split(total, 2)
    high[...] = parts[0]
    low[...] = parts[1]

    b = bias[...] * LOG2E
    lane = lax.broadcasted_iota(jnp.int32, b.shape, 1)
    for i in range(blocks):
        large[i].wait()
        for j in range(block):
            tail = jnp.where(lane == i * block + j, b, 0.0)
            parts = split(jnp.concatenate([absorb[i, :, j, :], tail], axis=1), 2)
            table[i * block + j, :, 0:depth] = parts[0]
            table[i * block + j, :, depth:double] = parts[1]


def prepare(absorb, bias, planck, share, stencil, weight, coarse):
    g, levels, feat = absorb.shape
    fine = stencil.shape[1]
    block = 8
    depth = feat + levels
    column = jax.ShapeDtypeStruct((g, coarse), f32)
    spread_table = jax.ShapeDtypeStruct((2 * coarse, fine), bf16)
    return pl.pallas_call(
        functools.partial(prepare_body, block),
        out_shape=(
            jax.ShapeDtypeStruct((levels, g, 2 * depth), bf16),
            column,
            column,
            spread_table,
            spread_table,
        ),
        in_specs=[HBM] * 6,
        out_specs=[VMEM] * 5,
        scratch_shapes=[
            pltpu.VMEM((levels // block, g, block, feat), f32),
            pltpu.VMEM(bias.shape, f32),
            pltpu.VMEM(planck.shape, f32),
            pltpu.VMEM(share.shape, f32),
            pltpu.VMEM(stencil.shape, jnp.int32),
            pltpu.VMEM(weight.shape, f32),
            pltpu.SemaphoreType.DMA((5 + levels // block,)),
        ],
        compiler_params=pltpu.CompilerParams(vmem_limit_bytes=28 * MIB),
        cost_estimate=pl.CostEstimate(
            flops=10 * g * levels * feat, bytes_accessed=8 * g * levels * depth, transcendentals=0
        ),
        name="prepare",
    )(*(stay(x) for x in (absorb, bias, planck, share, stencil, weight)))


def flux_body(block, scale, span, count, table, planck, share, *refs):
    chunks, outs, scratch = refs[:count], refs[count : 2 * count], refs[2 * count :]
    sweeps(block, scale, span, table, chunks, planck, share, outs, scratch)


def flux(table, planck, share, chunks, scale, span=None):
    levels, g, double = table.shape
    span = span or (0, g)
    g = span[1] - span[0]
    count, half = len(chunks), chunks[0].shape[1]
    block = 4 if count == 2 or 2 * g > table.shape[1] else 8
    return pl.pallas_call(
        functools.partial(flux_body, block, scale, span, count),
        out_shape=(jax.ShapeDtypeStruct((levels, half), f32),) * count,
        in_specs=[VMEM] * (3 + count),
        out_specs=(VMEM,) * count,
        scratch_shapes=sweep_scratch(block, g, levels, double // 2, count, half),
        compiler_params=pltpu.CompilerParams(vmem_limit_bytes=20 * MIB),
        cost_estimate=pl.CostEstimate(
            flops=3 * g * levels * double * count * half,
            bytes_accessed=2 * g * levels * double,
            transcendentals=3 * g * levels * count * half,
        ),
        name="flux",
    )(table, planck, share, *chunks)


def spread_body(own, first, second, parity, high, low, out):
    n = own.shape[1]
    lane = lax.broadcasted_iota(jnp.int32, own.shape, 1)
    late = jnp.where(lane >= n // 2, 1, 0)
    halo = jnp.where(late == parity[0], first[...], second[...])
    wide = jnp.concatenate([own[...], halo], axis=1)
    a, c = split(wide, 2)
    both = dot(jnp.concatenate([a, c], axis=0), high[...])
    m = a.shape[0]
    out[...] = both[0:m] + (dot(a, low[...]) + both[m : 2 * m])


def spread(own, first, second, parity, high, low):
    levels = own.shape[0]
    fine = high.shape[1]
    return pl.pallas_call(
        spread_body,
        out_shape=jax.ShapeDtypeStruct((levels, fine), f32),
        in_specs=[VMEM] * 3 + [pl.BlockSpec(memory_space=pltpu.SMEM)] + [VMEM] * 2,
        out_specs=VMEM,
        compiler_params=pltpu.CompilerParams(vmem_limit_bytes=16 * MIB),
        name="spread",
    )(own, first, second, parity, high, low)


def shards(
    state, cosine, grouping, sunlit, absorb, level_bias, planck, solar_share, stencil, stencil_weight
):
    fine, fields, levels = state.shape
    coarse = fine // 4
    n_sec = lax.axis_size("sec")
    devices = n_sec * lax.axis_size("col")
    columns = state.transpose(1, 2, 0).reshape(fields * levels, fine)
    rows = group(columns, cosine[None], grouping, sunlit)

    def swap(x, m):
        return lax.ppermute(x, "sec", [(i, i ^ m) for i in range(n_sec)])

    scale = 4.0 / (planck.shape[0] * n_sec)
    first, second = swap(rows, 1), swap(rows, 2)
    table, weight, share, near, far = prepare(
        absorb, level_bias, planck[None], solar_share[None], stencil, stencil_weight, coarse
    )
    later, table = lax.optimization_barrier((first, table))
    third = swap(later, 2)
    heats = flux(table, weight, share, [first, second], scale)
    third, table, *heats = lax.optimization_barrier((third, table, *heats))
    (heat,) = flux(table, weight, share, [third], scale)
    heat, table, rows, *heats = lax.optimization_barrier((heat, table, rows, *heats))
    (total,) = flux(table, weight, share, [rows], scale)
    total = swap(heats[0], 1) + swap(heat, 3) + swap(heats[1], 2) + total
    pairs = [(i, i ^ 1) for i in range(devices)]
    across = [(i, (i + 1) % devices if i % 2 else (i - 1) % devices) for i in range(devices)]
    second = lax.ppermute(total, ("sec", "col"), across)
    first = lax.ppermute(total, ("sec", "col"), pairs)
    parity = jnp.bitwise_and(lax.axis_index(("sec", "col")), 1).astype(jnp.int32).reshape(1)
    return spread(total, second, first, 1 - parity, near, far)


def solution(mesh):
    placed = (
        P(("sec", "col"), None, None),
        P(("sec", "col")),
        P(("sec", "col"), None),
        P(("sec", "col")),
        P("sec", None, None),
        P("sec", None),
        P("sec"),
        P("sec"),
        P(None, ("sec", "col")),
        P(None, ("sec", "col")),
    )
    return jax.shard_map(
        shards, mesh=mesh, in_specs=placed, out_specs=P(None, ("sec", "col")), check_vma=False
    )
```
